128 devices in a mesh: loc: 16 (over y, x), stream: 8 (over z, core).
Axes of the slice: x: 4, y: 4, z: 4, core: 2. Of those that a mesh axis runs over, the one named last changes fastest.
Arguments:
- latent: bfloat16 [49152, 1024], P(('loc', 'stream')), may hold values from -7 to 7
- observations: bfloat16 [8, 16, 16, 32, 1024], P('stream', 'loc'), may hold values from -7 to 7
- counts: int32 [8, 16, 16], P('stream', 'loc'), may hold values from 1 to 32, as said below
- cross_query: bfloat16 [1024, 1024], replicated, may hold values from -1 to 1
- cross_kv: bfloat16 [1024, 2048], replicated, may hold values from -1 to 1
- cross_out: bfloat16 [1024, 1024], replicated, may hold values from -0.1875 to 0.1875
- self_qkv: bfloat16 [1024, 3072], replicated, may hold values from -1 to 1
- self_out: bfloat16 [1024, 1024], replicated, may hold values from -0.1875 to 0.1875
- mlp_in: bfloat16 [1024, 4096], P(None, ('loc', 'stream')), may hold values from -0.1875 to 0.1875
- mlp_out: bfloat16 [1024, 4096], P(None, ('loc', 'stream')), may hold values from -0.09375 to 0.09375
Outputs:
- forecast: bfloat16 [49152, 1024], P(('loc', 'stream'))
The draws below stay inside these ranges and needn't reach their ends.
Inputs may be any that keep to these rules, and one draw needn't show every extreme that they name: `counts`: slots 0 to count - 1 of a block hold observations and the rest are padding; for every stream some section receives 32 rows from every ingest shard.
All inputs are finite; a program needn't handle non-finite values.
Results may differ from the reference program's by a relative error of at most 0.013.
Values may be sent and summed in bfloat16 or wider, within the bound.
A program may use at most 192 MiB of HBM per device.

```python
import math
import jax
import jax.numpy as jnp
from jax import lax

D = 1024
HEADS = 16
FF = 4096
WIN = 512
NODE_DEV = 384
CAP = 32
NODES = 49152
N_LOC = 16
N_STREAM = 8


def base_weight(key, fold_value, array_shape):
    noise_draw = jax.random.normal(jax.random.fold_in(key, fold_value), array_shape, jnp.float32)
    return jnp.clip(noise_draw, -6.0, 6.0) / math.sqrt(array_shape[0])


def feature_rows(key, fold_value, array_shape):
    noise_draw = jax.random.normal(jax.random.fold_in(key, fold_value), array_shape, jnp.float32)
    return jnp.clip(noise_draw, -6.0, 6.0)


def draw_latent(key, part):
    return feature_rows(key, 701, (NODES, D)).astype(jnp.bfloat16)


def draw_observations(key, part):
    return feature_rows(key, 711, (N_STREAM, N_LOC, N_LOC, CAP, D)).astype(jnp.bfloat16)


def draw_cross_query(key, part):
    weights = base_weight(key, 721, (D, D))
    return weights.astype(jnp.bfloat16)


def draw_cross_kv(key, part):
    weights = base_weight(key, 722, (D, 2 * D))
    return weights.astype(jnp.bfloat16)


def draw_self_qkv(key, part):
    weights = base_weight(key, 723, (D, 3 * D))
    return weights.astype(jnp.bfloat16)


def draw_counts(key, part):
    base_key = jax.random.fold_in(key, 11)
    load_key, fill_key, full_key = jax.random.split(base_key, 3)
    section_load = jax.random.randint(load_key, (N_STREAM, 1, N_LOC), 1, 5)
    raw_fill = jax.random.randint(fill_key, (N_STREAM, N_LOC, N_LOC), 0, CAP)
    filled = 1 + raw_fill * section_load // 4
    full_section = jax.random.randint(full_key, (N_STREAM, 1, 1), 0, N_LOC)
    section_index = lax.broadcasted_iota(jnp.int32, (N_STREAM, N_LOC, N_LOC), 2)
    filled = jnp.where(section_index == full_section, CAP, filled)
    return filled.astype(jnp.int32)


def levels(stream_key, shape, cuts, low, high):
    gain, own = 1.0, jax.random.fold_in(stream_key, 6)
    for axis_at, shards_of in cuts:
        draws = jnp.exp(jax.random.uniform(jax.random.fold_in(own, axis_at), (shards_of,), jnp.float32, low / len(cuts), high / len(cuts)))
        gain = gain * jnp.repeat(draws, shape[axis_at] // shards_of).reshape([-1 if axis == axis_at else 1 for axis in range(len(shape))])
    return gain


def noise(own_key, dims, width, limit, cuts=(), kind=jnp.bfloat16):
    values = jax.random.normal(own_key, dims, jnp.float32) * width
    if len(cuts) > 0:
        values = levels(own_key, dims, cuts, -0.22, 0.18) * values
    return jnp.clip(values, min=-limit, max=limit).astype(kind)


def setup_inputs(seed: int = 0) -> dict:
    key_of = jax.random.split(jax.random.key(seed), 11)
    return {
        "latent": draw_latent(jax.random.fold_in(key_of[10], 71), 0),
        "observations": draw_observations(jax.random.fold_in(key_of[10], 71), 0),
        "counts": draw_counts(jax.random.fold_in(key_of[10], 71), 0),
        "cross_query": draw_cross_query(jax.random.fold_in(key_of[10], 71), 0),
        "cross_kv": draw_cross_kv(jax.random.fold_in(key_of[10], 71), 0),
        "cross_out": noise(key_of[5], (D, D), D ** -0.5, 0.1875),
        "self_qkv": draw_self_qkv(jax.random.fold_in(key_of[10], 71), 0),
        "self_out": noise(key_of[7], (D, D), D ** -0.5, 0.1875),
        "mlp_in": noise(key_of[8], (D, FF), D ** -0.5, 0.1875, ((1, 128),)),
        "mlp_out": noise(key_of[9], (D, FF), FF ** -0.5, 0.09375, ((1, 128),)),
    }


EPSILON = 1e-06
MASKED = -1e+30

def rms_norm(tensor):
    floats = tensor.astype(jnp.float32)
    return (floats * lax.rsqrt(lax.optimization_barrier(jnp.mean(floats * floats, axis=-1, keepdims=True)) + EPSILON)).astype(jnp.bfloat16)

def masked_attention(queries, key_rows, value_rows, allowed):
    row_count = queries.shape[0]
    feat_width = queries.shape[1]
    head_width = feat_width // HEADS
    query_per_head = queries.astype(jnp.float32).reshape(row_count, HEADS, head_width)
    key_per_head = key_rows.astype(jnp.float32).reshape(key_rows.shape[0], HEADS, head_width)
    value_per_head = value_rows.astype(jnp.float32).reshape(value_rows.shape[0], HEADS, head_width)
    score_matrix = jnp.einsum('jsv,esv->sje', query_per_head, key_per_head) * (1.0 / math.sqrt(head_width))
    score_matrix = jnp.where(allowed[None], score_matrix, MASKED)
    row_max = lax.optimization_barrier(jnp.max(score_matrix, axis=2, keepdims=True))
    exp_terms = jnp.where(allowed[None], jnp.exp(score_matrix - row_max), 0.0)
    row_sum = lax.optimization_barrier(jnp.sum(exp_terms, axis=2))
    rounded_values = lax.optimization_barrier(exp_terms.astype(jnp.bfloat16))
    mixed_output = jnp.einsum('lsu,uly->sly', rounded_values.astype(jnp.float32), value_per_head)
    mixed_output = mixed_output / jnp.transpose(row_sum)[:, :, None]
    return mixed_output.reshape(row_count, feat_width).astype(jnp.bfloat16)

def reference(latent, observations, counts, cross_query, cross_kv, cross_out, self_qkv, self_out, mlp_in, mlp_out):
    feat_width = latent.shape[1]
    slot_index = lax.broadcasted_iota(jnp.int32, observations.shape[:4], 3)
    live = slot_index < counts[..., None]
    obs_kv = jnp.dot(rms_norm(observations.reshape(-1, feat_width)), cross_kv, preferred_element_type=jnp.float32).astype(jnp.bfloat16)
    obs_kv = obs_kv.reshape(N_STREAM, N_LOC, N_LOC, CAP, 2 * feat_width)
    queries = jnp.dot(rms_norm(latent), cross_query, preferred_element_type=jnp.float32).astype(jnp.bfloat16)
    block_total = N_LOC * N_STREAM

    def cross_block(block_index):
        section = block_index // N_STREAM
        section_kv = lax.dynamic_index_in_dim(obs_kv, section, 2, keepdims=False).reshape(-1, 2 * feat_width)
        section_live = lax.dynamic_index_in_dim(live, section, 2, keepdims=False).reshape(-1)
        block_rows = lax.dynamic_slice_in_dim(queries, (block_index * NODE_DEV).astype(jnp.int32), NODE_DEV, 0)
        allowed = jnp.broadcast_to(section_live[None, :], (NODE_DEV, section_live.shape[0]))
        return masked_attention(block_rows, section_kv[:, :feat_width], section_kv[:, feat_width:], allowed)
    cross_ctx = lax.map(cross_block, jnp.arange(block_total, dtype=jnp.int32)).reshape(-1, feat_width)
    after_cross = (latent.astype(jnp.float32) + jnp.dot(cross_ctx, cross_out, preferred_element_type=jnp.float32)).astype(jnp.bfloat16)
    self_proj = jnp.dot(rms_norm(after_cross), self_qkv, preferred_element_type=jnp.float32).astype(jnp.bfloat16)
    half_win = WIN // 2
    padded_kv = jnp.pad(self_proj[:, feat_width:], ((half_win, half_win), (0, 0)))

    def window_block(block_index):
        offset = (block_index * NODE_DEV).astype(jnp.int32)
        block_rows = lax.dynamic_slice_in_dim(self_proj[:, :feat_width], offset, NODE_DEV, 0)
        window_kv = lax.dynamic_slice_in_dim(padded_kv, offset, NODE_DEV + 2 * half_win, 0)
        query_pos = offset + lax.broadcasted_iota(jnp.int32, (NODE_DEV, 1), 0)
        key_pos = offset - half_win + lax.broadcasted_iota(jnp.int32, (1, NODE_DEV + 2 * half_win), 1)
        allowed = (jnp.abs(query_pos - key_pos) <= half_win) & (key_pos >= 0) & (key_pos < NODES)
        self_ctx = masked_attention(block_rows, window_kv[:, :feat_width], window_kv[:, feat_width:], allowed)
        residual = lax.dynamic_slice_in_dim(after_cross, offset, NODE_DEV, 0)
        after_self = (residual.astype(jnp.float32) + jnp.dot(self_ctx, self_out, preferred_element_type=jnp.float32)).astype(jnp.bfloat16)
        hidden = jax.nn.gelu(jnp.dot(rms_norm(after_self), mlp_in, preferred_element_type=jnp.float32), approximate=True).astype(jnp.bfloat16)
        grown = jnp.dot(hidden, jnp.transpose(mlp_out), preferred_element_type=jnp.float32)
        return (after_self.astype(jnp.float32) + grown).astype(jnp.bfloat16)
    return lax.map(window_block, jnp.arange(block_total, dtype=jnp.int32)).reshape(-1, feat_width)
```

```python
import functools
import math

import jax
import jax.numpy as jnp
from jax import lax
from jax.experimental import pallas as pl
from jax.experimental.pallas import tpu as pltpu
from jax.sharding import Mesh
from jax.sharding import PartitionSpec as P

HEADS = 16
HEAD = 64
PAIR = 128
GROUPS = 8
WIN = 512
LOC = 16
CAP = 32
STREAM = ("s0", "s1")
LOC_STREAM = ("loc", "s0", "s1")
EPSILON = 1e-06
MASKED = -1e30
PADDING = 1e30
PADDING_FROM = 1e29
QSCALE = math.log2(math.e) / math.sqrt(HEAD)
MESH = pl.DeviceIdType.MESH
F32 = jnp.float32
BF16 = jnp.bfloat16
NT = (((1,), (1,)), ((), ()))
VMEM_LIMIT = 56 << 20


def params(**more):
    return pltpu.CompilerParams(vmem_limit_bytes=VMEM_LIMIT, **more)


def rms_norm(tensor):
    floats = tensor.astype(F32)
    return (floats * lax.rsqrt(jnp.mean(floats * floats, axis=-1, keepdims=True) + EPSILON)).astype(
        BF16
    )


def project_kernel(counts, obs, latent, wk, wv, wq, kv_out, q_out, xn, ln):
    @pl.when(pl.program_id(0) == 0)
    def _():
        xn[...] = rms_norm(obs[...])
        ln[...] = rms_norm(latent[...])

    q = (jnp.dot(ln[...], wq[...], preferred_element_type=F32) * QSCALE).astype(BF16)
    k = jnp.dot(xn[...], wk[...], preferred_element_type=F32)
    v = jnp.dot(xn[...], wv[...], preferred_element_type=F32)
    slot = lax.broadcasted_iota(jnp.int32, (CAP, PAIR), 0)
    for s in range(LOC):
        live = slot < counts[s]
        rows = slice(s * CAP, (s + 1) * CAP)
        for g in range(2):
            columns = slice(g * PAIR, (g + 1) * PAIR)
            kv_out[s, g, :, 0:PAIR] = jnp.where(live, k[rows, columns], PADDING).astype(BF16)
            kv_out[s, g, :, PAIR:] = jnp.where(live, v[rows, columns], PADDING).astype(BF16)
    for g in range(2):
        q_out[g] = q[:, g * PAIR : (g + 1) * PAIR]


def project(counts, obs, latent, cross_kv, cross_query):
    rows, width = obs.shape
    nodes = latent.shape[0]
    step = 2 * PAIR
    steps = width // step
    return pl.pallas_call(
        project_kernel,
        grid=(steps,),
        out_shape=(
            jax.ShapeDtypeStruct((LOC, GROUPS, CAP, 2 * PAIR), BF16),
            jax.ShapeDtypeStruct((GROUPS, nodes, PAIR), BF16),
        ),
        in_specs=[
            pl.BlockSpec(memory_space=pltpu.SMEM),
            pl.BlockSpec((rows, width), lambda j: (0, 0)),
            pl.BlockSpec((nodes, width), lambda j: (0, 0)),
            pl.BlockSpec((width, step), lambda j: (0, j)),
            pl.BlockSpec((width, step), lambda j: (0, j + steps)),
            pl.BlockSpec((width, step), lambda j: (0, j)),
        ],
        out_specs=(
            pl.BlockSpec((LOC, 2, CAP, 2 * PAIR), lambda j: (0, j, 0, 0)),
            pl.BlockSpec((2, nodes, PAIR), lambda j: (j, 0, 0)),
        ),
        scratch_shapes=[pltpu.VMEM((rows, width), BF16), pltpu.VMEM((nodes, width), BF16)],
        compiler_params=params(),
        name="project",
    )(counts, obs, latent, cross_kv, cross_kv, cross_query)


def exchange_kernel(kv, q, kv_here, q_here, kv_send, kv_recv, q_send, q_recv):
    loc = lax.axis_index("loc")
    me = lax.axis_index("s0") * 2 + lax.axis_index("s1")
    mine = loc * GROUPS + me
    pltpu.make_async_copy(q.at[me], q_here.at[me], q_recv).start()
    pltpu.make_async_copy(kv.at[mine], kv_here.at[me * LOC + loc], kv_recv).start()

    @pl.loop(1, GROUPS)
    def _(d):
        to = lax.rem(me + d, GROUPS)
        pltpu.make_async_remote_copy(
            q.at[to],
            q_here.at[me],
            q_send,
            q_recv,
            device_id=(loc, to // 2, lax.rem(to, 2)),
            device_id_type=MESH,
        ).start()

    @pl.loop(1, LOC * GROUPS)
    def _(d):
        to = lax.rem(mine + d, LOC * GROUPS)
        section = to // GROUPS
        group = lax.rem(to, GROUPS)
        pltpu.make_async_remote_copy(
            kv.at[to],
            kv_here.at[me * LOC + loc],
            kv_send,
            kv_recv,
            device_id=(section, group // 2, lax.rem(group, 2)),
            device_id_type=MESH,
        ).start()

    pltpu.make_async_copy(q.at[pl.ds(0, GROUPS - 1)], q_here.at[pl.ds(0, GROUPS - 1)], q_send).wait()
    pltpu.make_async_copy(q, q_here, q_recv).wait()

    sent = pl.ds(0, LOC * GROUPS - 1)
    pltpu.make_async_copy(kv.at[sent], kv_here.at[sent], kv_send).wait()
    pltpu.make_async_copy(kv_here, kv_here, kv_recv).wait()


def exchange(kv, q):
    return pl.pallas_call(
        exchange_kernel,
        out_shape=(
            jax.ShapeDtypeStruct(kv.shape, BF16),
            jax.ShapeDtypeStruct(q.shape, BF16),
        ),
        in_specs=[pl.BlockSpec(memory_space=pl.ANY)] * 2,
        out_specs=(pl.BlockSpec(memory_space=pl.ANY),) * 2,
        scratch_shapes=[pltpu.SemaphoreType.DMA] * 4,
        compiler_params=params(has_side_effects=True),
        name="exchange",
    )(kv, q)


def give_back_kernel(ctx, ctx_here, send, recv):
    loc = lax.axis_index("loc")
    me = lax.axis_index("s0") * 2 + lax.axis_index("s1")
    pltpu.make_async_copy(ctx.at[me], ctx_here.at[me], recv).start()

    @pl.loop(1, GROUPS)
    def _(d):
        to = lax.rem(me + d, GROUPS)
        pltpu.make_async_remote_copy(
            ctx.at[to],
            ctx_here.at[me],
            send,
            recv,
            device_id=(loc, to // 2, lax.rem(to, 2)),
            device_id_type=MESH,
        ).start()

    pltpu.make_async_copy(ctx.at[pl.ds(0, GROUPS - 1)], ctx_here.at[pl.ds(0, GROUPS - 1)], send).wait()
    pltpu.make_async_copy(ctx, ctx_here, recv).wait()


def give_back(ctx):
    return pl.pallas_call(
        give_back_kernel,
        out_shape=jax.ShapeDtypeStruct(ctx.shape, BF16),
        in_specs=[pl.BlockSpec(memory_space=pl.ANY)],
        out_specs=pl.BlockSpec(memory_space=pl.ANY),
        scratch_shapes=[pltpu.SemaphoreType.DMA] * 2,
        compiler_params=params(has_side_effects=True),
        name="give_back",
    )(ctx)


def lane_max(scores, width):
    top = scores[:, 0:PAIR]
    for c in range(1, width // PAIR):
        top = jnp.maximum(top, scores[:, c * PAIR : (c + 1) * PAIR])
    return top


def cross_kernel(tile, kv, q, out, k0, k1, v0, v1, s0, s1):
    rows = kv.shape[0]
    block = q.shape[0]

    @pl.when(pl.program_id(0) == 0)
    def _():
        prep = 512
        lane = lax.broadcasted_iota(jnp.int32, (prep, PAIR), 1)
        low = lane < HEAD

        @pl.loop(0, rows // prep)
        def _(b):
            at = pl.ds(pl.multiple_of(b * prep, prep), prep)
            key = kv[at, 0:PAIR].astype(F32)
            value = kv[at, PAIR:].astype(F32)
            live = key < PADDING_FROM
            bias = jnp.where(live, 0.0, MASKED)
            key = jnp.where(live, key, 0.0)
            value = jnp.where(live, value, 0.0)
            first = jnp.where(low, key, jnp.where(lane == HEAD, bias, 0.0))
            second = jnp.where(low, jnp.where(lane == 0, bias, 0.0), key)
            k0[:, at] = jnp.transpose(first).astype(BF16)
            k1[:, at] = jnp.transpose(second).astype(BF16)
            v0[at, :] = jnp.where(low, value, 1.0).astype(BF16)
            v1[at, :] = jnp.where(low, 1.0, value).astype(BF16)

    lane = lax.broadcasted_iota(jnp.int32, (block, PAIR), 1)
    low = lane < HEAD
    both = q[...].astype(F32)
    q0 = jnp.where(low, both, jnp.where(lane == HEAD, 1.0, 0.0)).astype(BF16)
    q1 = jnp.where(low, jnp.where(lane == 0, 1.0, 0.0), both).astype(BF16)
    lowest = jnp.full((block, PAIR), -3e38, F32)

    def score(b, tops):
        at = pl.ds(pl.multiple_of(b * tile, tile), tile)
        a0 = jnp.dot(q0, k0[:, at], preferred_element_type=F32)
        s0[:, at] = a0
        a1 = jnp.dot(q1, k1[:, at], preferred_element_type=F32)
        s1[:, at] = a1
        return (
            jnp.maximum(tops[0], lane_max(a0, tile)),
            jnp.maximum(tops[1], lane_max(a1, tile)),
        )

    tops = lax.fori_loop(0, rows // tile, score, (lowest, lowest))
    m0 = jnp.max(tops[0], axis=1, keepdims=True)
    m1 = jnp.max(tops[1], axis=1, keepdims=True)

    def mix(b, totals):
        at = pl.ds(pl.multiple_of(b * tile, tile), tile)
        p0 = jnp.exp2(s0[:, at] - m0).astype(BF16)
        p1 = jnp.exp2(s1[:, at] - m1).astype(BF16)
        return (
            totals[0] + jnp.dot(p0, v0[at, :], preferred_element_type=F32),
            totals[1] + jnp.dot(p1, v1[at, :], preferred_element_type=F32),
        )

    zero = jnp.zeros((block, PAIR), F32)
    t0, t1 = lax.fori_loop(0, rows // tile, mix, (zero, zero))
    sums = pltpu.roll(jnp.where(low, t1, t0), HEAD, 1)
    out[...] = (jnp.where(low, t0, t1) / sums).astype(BF16)


def cross_attention(kv, q, block=256, tile=512):
    rows = kv.shape[0]
    nodes = q.shape[0]
    return pl.pallas_call(
        functools.partial(cross_kernel, tile),
        grid=(nodes // block,),
        out_shape=jax.ShapeDtypeStruct(q.shape, BF16),
        in_specs=[
            pl.BlockSpec((rows, 2 * PAIR), lambda j: (0, 0)),
            pl.BlockSpec((block, PAIR), lambda j: (j, 0)),
        ],
        out_specs=pl.BlockSpec((block, PAIR), lambda j: (j, 0)),
        scratch_shapes=[
            pltpu.VMEM((PAIR, rows), BF16),
            pltpu.VMEM((PAIR, rows), BF16),
            pltpu.VMEM((rows, PAIR), BF16),
            pltpu.VMEM((rows, PAIR), BF16),
            pltpu.VMEM((block, rows), F32),
            pltpu.VMEM((block, rows), F32),
        ],
        compiler_params=params(),
        name="cross_attention",
    )(kv, q)


def window_kernel(block, edge, q, key_low, key_own, key_high, value_low, value_own, value_high, out, bias):
    nodes = q.shape[0]
    half = key_low.shape[0]
    wide = block + 2 * half
    first = edge[0]
    last = edge[1]

    @pl.when(pl.program_id(0) == 0)
    def _():
        row = lax.broadcasted_iota(jnp.int32, (block, wide), 0)
        column = lax.broadcasted_iota(jnp.int32, (block, wide), 1)
        near = (column >= row) & (column <= row + 2 * half)
        for b in range(nodes // block):
            there = (column + b * block >= first) & (column + b * block < last)
            bias[b] = jnp.where(near & there, 0.0, MASKED)

    keys = jnp.concatenate([key_low[...], key_own[...], key_high[...]], axis=0)
    values = jnp.concatenate([value_low[...], value_own[...], value_high[...]], axis=0).astype(F32)
    low_keys = lax.broadcasted_iota(jnp.int32, values.shape, 1) < HEAD
    v0 = jnp.where(low_keys, values, 1.0).astype(BF16)
    v1 = jnp.where(low_keys, 1.0, values).astype(BF16)
    low = lax.broadcasted_iota(jnp.int32, (block, PAIR), 1) < HEAD
    for b in range(nodes // block):
        both = q[b * block : (b + 1) * block, :].astype(F32)
        q0 = jnp.where(low, both, 0.0).astype(BF16)
        q1 = jnp.where(low, 0.0, both).astype(BF16)
        near = slice(b * block, b * block + wide)
        a0 = lax.dot_general(q0, keys[near], NT, preferred_element_type=F32) + bias[b]
        a1 = lax.dot_general(q1, keys[near], NT, preferred_element_type=F32) + bias[b]
        p0 = jnp.exp2(a0 - jnp.max(a0, axis=1, keepdims=True)).astype(BF16)
        p1 = jnp.exp2(a1 - jnp.max(a1, axis=1, keepdims=True)).astype(BF16)
        t0 = jnp.dot(p0, v0[near], preferred_element_type=F32)
        t1 = jnp.dot(p1, v1[near], preferred_element_type=F32)
        sums = pltpu.roll(jnp.where(low, t1, t0), HEAD, 1)
        out[b * block : (b + 1) * block, :] = (jnp.where(low, t0, t1) / sums).astype(BF16)


def window_attention(edge, proj, low, high, block=128):
    nodes = proj.shape[0]
    half = low.shape[0]
    pairs = GROUPS
    return pl.pallas_call(
        functools.partial(window_kernel, block),
        grid=(pairs,),
        out_shape=jax.ShapeDtypeStruct((nodes, pairs * PAIR), BF16),
        in_specs=[
            pl.BlockSpec(memory_space=pltpu.SMEM),
            pl.BlockSpec((nodes, PAIR), lambda j: (0, j)),
            pl.BlockSpec((half, PAIR), lambda j: (0, j)),
            pl.BlockSpec((nodes, PAIR), lambda j: (0, j + pairs)),
            pl.BlockSpec((half, PAIR), lambda j: (0, j)),
            pl.BlockSpec((half, PAIR), lambda j: (0, j + pairs)),
            pl.BlockSpec((nodes, PAIR), lambda j: (0, j + 2 * pairs)),
            pl.BlockSpec((half, PAIR), lambda j: (0, j + pairs)),
        ],
        out_specs=pl.BlockSpec((nodes, PAIR), lambda j: (0, j)),
        scratch_shapes=[pltpu.VMEM((nodes // block, block, block + 2 * half), F32)],
        compiler_params=params(),
        name="window_attention",
    )(edge, proj, low, proj, high, low, proj, high)


def shards(
    latent,
    observations,
    counts,
    cross_query,
    cross_kv,
    cross_out,
    self_qkv,
    self_out,
    mlp_in,
    mlp_out,
):
    nodes, width = latent.shape
    weight_in = lax.all_gather(mlp_in, LOC_STREAM, axis=1, tiled=True)
    weight_back = lax.all_gather(mlp_out, LOC_STREAM, axis=1, tiled=True)
    kv, q = project(
        counts.reshape(-1), observations.reshape(-1, width), latent, cross_kv, cross_query
    )
    kv_here, q_here = exchange(kv.reshape(LOC * GROUPS, CAP, 2 * PAIR), q)
    ctx = cross_attention(
        kv_here.reshape(-1, 2 * PAIR), q_here.reshape(-1, PAIR)
    )
    ctx = give_back(ctx.reshape(GROUPS, nodes, PAIR))
    cross_ctx = jnp.transpose(ctx, (1, 0, 2)).reshape(nodes, width)
    after_cross = (
        latent.astype(F32) + jnp.dot(cross_ctx, cross_out, preferred_element_type=F32)
    ).astype(BF16)
    proj = jnp.dot(rms_norm(after_cross), self_qkv, preferred_element_type=F32)
    scale = jnp.where(lax.broadcasted_iota(jnp.int32, (1, 3 * width), 1) < width, QSCALE, 1.0)
    proj = (proj * scale).astype(BF16)
    half = WIN // 2
    me = lax.axis_index(LOC_STREAM)
    count = LOC * GROUPS
    up = [(i, i + 1) for i in range(count - 1)]
    down = [(i + 1, i) for i in range(count - 1)]
    low = lax.ppermute(proj[nodes - half :, width:], LOC_STREAM, up)
    high = lax.ppermute(proj[:half, width:], LOC_STREAM, down)
    edge = jnp.stack(
        [jnp.where(me == 0, half, 0), jnp.where(me == count - 1, half + nodes, nodes + WIN)]
    ).astype(jnp.int32)
    self_ctx = window_attention(edge, proj, low, high)
    after_self = (
        after_cross.astype(F32) + jnp.dot(self_ctx, self_out, preferred_element_type=F32)
    ).astype(BF16)
    hidden = jax.nn.gelu(
        jnp.dot(rms_norm(after_self), weight_in, preferred_element_type=F32), approximate=True
    ).astype(BF16)
    mlp_sum = lax.dot_general(hidden, weight_back, NT, preferred_element_type=F32)
    return (after_self.astype(F32) + mlp_sum).astype(BF16)


def solution(mesh):
    finer = Mesh(mesh.devices.reshape(LOC, 4, 2), LOC_STREAM)
    return jax.shard_map(
        shards,
        mesh=finer,
        in_specs=(
            P(LOC_STREAM, None),
            P(STREAM, "loc", None, None, None),
            P(STREAM, "loc", None),
            P(),
            P(),
            P(),
            P(),
            P(),
            P(None, LOC_STREAM),
            P(None, LOC_STREAM),
        ),
        out_specs=P(LOC_STREAM, None),
        check_vma=False,
    )
```

```python
import functools
import math

import jax
import jax.numpy as jnp
from jax import lax
from jax.experimental import pallas as pl
from jax.experimental.pallas import tpu as pltpu
from jax.sharding import Mesh
from jax.sharding import PartitionSpec as P

HEADS = 16
HEAD = 64
PAIR = 128
GROUPS = 8
WIN = 512
LOC = 16
CAP = 32
STREAM = ("s0", "s1")
LOC_STREAM = ("loc", "s0", "s1")
EPSILON = 1e-06
MASKED = -1e30
PADDING = 1e30
PADDING_FROM = 1e29
QSCALE = math.log2(math.e) / math.sqrt(HEAD)
MESH = pl.DeviceIdType.MESH
F32 = jnp.float32
BF16 = jnp.bfloat16
NT = (((1,), (1,)), ((), ()))
VMEM_LIMIT = 56 << 20


def params(**more):
    return pltpu.CompilerParams(vmem_limit_bytes=VMEM_LIMIT, **more)


def rms_norm(tensor):
    floats = tensor.astype(F32)
    return (floats * lax.rsqrt(jnp.mean(floats * floats, axis=-1, keepdims=True) + EPSILON)).astype(
        BF16
    )


def project_kernel(counts, obs, latent, wk, wv, wq, kv_out, q_out, xn, ln):
    @pl.when(pl.program_id(0) == 0)
    def _():
        xn[...] = rms_norm(obs[...])
        ln[...] = rms_norm(latent[...])

    q = (jnp.dot(ln[...], wq[...], preferred_element_type=F32) * QSCALE).astype(BF16)
    k = jnp.dot(xn[...], wk[...], preferred_element_type=F32)
    v = jnp.dot(xn[...], wv[...], preferred_element_type=F32)
    slot = lax.broadcasted_iota(jnp.int32, (CAP, PAIR), 0)
    for s in range(LOC):
        live = slot < counts[s]
        rows = slice(s * CAP, (s + 1) * CAP)
        for g in range(2):
            columns = slice(g * PAIR, (g + 1) * PAIR)
            kv_out[s, g, :, 0:PAIR] = jnp.where(live, k[rows, columns], PADDING).astype(BF16)
            kv_out[s, g, :, PAIR:] = jnp.where(live, v[rows, columns], PADDING).astype(BF16)
    for g in range(2):
        q_out[g] = q[:, g * PAIR : (g + 1) * PAIR]


def project(counts, obs, latent, cross_kv, cross_query):
    rows, width = obs.shape
    nodes = latent.shape[0]
    step = 2 * PAIR
    steps = width // step
    return pl.pallas_call(
        project_kernel,
        grid=(steps,),
        out_shape=(
            jax.ShapeDtypeStruct((LOC, GROUPS, CAP, 2 * PAIR), BF16),
            jax.ShapeDtypeStruct((GROUPS, nodes, PAIR), BF16),
        ),
        in_specs=[
            pl.BlockSpec(memory_space=pltpu.SMEM),
            pl.BlockSpec((rows, width), lambda j: (0, 0)),
            pl.BlockSpec((nodes, width), lambda j: (0, 0)),
            pl.BlockSpec((width, step), lambda j: (0, j)),
            pl.BlockSpec((width, step), lambda j: (0, j + steps)),
            pl.BlockSpec((width, step), lambda j: (0, j)),
        ],
        out_specs=(
            pl.BlockSpec((LOC, 2, CAP, 2 * PAIR), lambda j: (0, j, 0, 0)),
            pl.BlockSpec((2, nodes, PAIR), lambda j: (j, 0, 0)),
        ),
        scratch_shapes=[pltpu.VMEM((rows, width), BF16), pltpu.VMEM((nodes, width), BF16)],
        compiler_params=params(),
        name="project",
    )(counts, obs, latent, cross_kv, cross_kv, cross_query)


def exchange_kernel(kv, q, kv_here, q_here, kv_send, kv_recv, q_send, q_recv):
    loc = lax.axis_index("loc")
    me = lax.axis_index("s0") * 2 + lax.axis_index("s1")
    mine = loc * GROUPS + me
    pltpu.make_async_copy(q.at[me], q_here.at[me], q_recv).start()
    pltpu.make_async_copy(kv.at[mine], kv_here.at[me * LOC + loc], kv_recv).start()

    @pl.loop(1, GROUPS)
    def _(d):
        to = lax.rem(me + d, GROUPS)
        pltpu.make_async_remote_copy(
            q.at[to],
            q_here.at[me],
            q_send,
            q_recv,
            device_id=(loc, to // 2, lax.rem(to, 2)),
            device_id_type=MESH,
        ).start()

    @pl.loop(1, LOC * GROUPS)
    def _(d):
        to = lax.rem(mine + d, LOC * GROUPS)
        section = to // GROUPS
        group = lax.rem(to, GROUPS)
        pltpu.make_async_remote_copy(
            kv.at[to],
            kv_here.at[me * LOC + loc],
            kv_send,
            kv_recv,
            device_id=(section, group // 2, lax.rem(group, 2)),
            device_id_type=MESH,
        ).start()

    pltpu.make_async_copy(q.at[pl.ds(0, GROUPS - 1)], q_here.at[pl.ds(0, GROUPS - 1)], q_send).wait()
    pltpu.make_async_copy(q, q_here, q_recv).wait()

    sent = pl.ds(0, LOC * GROUPS - 1)
    pltpu.make_async_copy(kv.at[sent], kv_here.at[sent], kv_send).wait()
    pltpu.make_async_copy(kv_here, kv_here, kv_recv).wait()


def exchange(kv, q):
    return pl.pallas_call(
        exchange_kernel,
        out_shape=(
            jax.ShapeDtypeStruct(kv.shape, BF16),
            jax.ShapeDtypeStruct(q.shape, BF16),
        ),
        in_specs=[pl.BlockSpec(memory_space=pl.ANY)] * 2,
        out_specs=(pl.BlockSpec(memory_space=pl.ANY),) * 2,
        scratch_shapes=[pltpu.SemaphoreType.DMA] * 4,
        compiler_params=params(has_side_effects=True),
        name="exchange",
    )(kv, q)


def give_back_kernel(ctx, ctx_here, send, recv):
    loc = lax.axis_index("loc")
    me = lax.axis_index("s0") * 2 + lax.axis_index("s1")
    pltpu.make_async_copy(ctx.at[me], ctx_here.at[me], recv).start()

    @pl.loop(1, GROUPS)
    def _(d):
        to = lax.rem(me + d, GROUPS)
        pltpu.make_async_remote_copy(
            ctx.at[to],
            ctx_here.at[me],
            send,
            recv,
            device_id=(loc, to // 2, lax.rem(to, 2)),
            device_id_type=MESH,
        ).start()

    pltpu.make_async_copy(ctx.at[pl.ds(0, GROUPS - 1)], ctx_here.at[pl.ds(0, GROUPS - 1)], send).wait()
    pltpu.make_async_copy(ctx, ctx_here, recv).wait()


def give_back(ctx):
    return pl.pallas_call(
        give_back_kernel,
        out_shape=jax.ShapeDtypeStruct(ctx.shape, BF16),
        in_specs=[pl.BlockSpec(memory_space=pl.ANY)],
        out_specs=pl.BlockSpec(memory_space=pl.ANY),
        scratch_shapes=[pltpu.SemaphoreType.DMA] * 2,
        compiler_params=params(has_side_effects=True),
        name="give_back",
    )(ctx)


PACK = 512
SIZES = (1024, 1536, 1792, 2048, 2304, 2560, 2816, 3072, 3584, 4096)
SPARE = 1024


def lane_max(scores, width):
    top = scores[:, 0:PAIR]
    for c in range(1, width // PAIR):
        top = jnp.maximum(top, scores[:, c * PAIR : (c + 1) * PAIR])
    return top


def pack_rows(kv, packed):
    row = lax.broadcasted_iota(jnp.int32, (PACK, PACK), 0)
    column = lax.broadcasted_iota(jnp.int32, (PACK, PACK), 1)
    slot = lax.broadcasted_iota(jnp.int32, (PACK, 2 * PAIR), 0)
    ones = jnp.ones((8, PACK), BF16)
    end = 0
    for g in range(kv.shape[0] // PACK):
        rows = kv[g * PACK : (g + 1) * PACK, :]
        live = rows[:, 0:1].astype(F32) < PADDING_FROM
        number = jnp.sum(live.astype(F32)).astype(jnp.int32)
        before = jnp.dot(ones, (live & (row < column)).astype(BF16), preferred_element_type=F32)
        itself = jnp.dot(ones, (live & (row == column)).astype(BF16), preferred_element_type=F32)
        place = jnp.where(itself > 0.5, before, -1.0)[0:1, :].astype(jnp.int32)
        pick = (place == row).astype(BF16)
        found = jnp.dot(pick, rows, preferred_element_type=F32)
        packed[pl.ds(pl.multiple_of(end, 16), PACK), :] = jnp.where(
            slot < number, found, PADDING
        ).astype(BF16)
        end = end + (number + 15) // 16 * 16
    packed[pl.ds(pl.multiple_of(end, 16), SPARE), :] = jnp.full((SPARE, 2 * PAIR), PADDING, BF16)
    return end


def cross_kernel(kv, q, out, packed, k0, k1, v0, v1, s0, s1, length):
    block = q.shape[0]

    @pl.when(pl.program_id(0) == 0)
    def _():
        end = pack_rows(kv, packed)
        length[0] = end
        lane = lax.broadcasted_iota(jnp.int32, (PACK, PAIR), 1)
        low = lane < HEAD

        @pl.loop(0, jnp.maximum((end + PACK - 1) // PACK, SIZES[0] // PACK))
        def _(b):
            at = pl.ds(pl.multiple_of(b * PACK, PACK), PACK)
            key = packed[at, 0:PAIR].astype(F32)
            value = packed[at, PAIR:].astype(F32)
            live = key < PADDING_FROM
            bias = jnp.where(live, 0.0, MASKED)
            key = jnp.where(live, key, 0.0)
            value = jnp.where(live, value, 0.0)
            first = jnp.where(low, key, jnp.where(lane == HEAD, bias, 0.0))
            second = jnp.where(low, jnp.where(lane == 0, bias, 0.0), key)
            k0[:, at] = jnp.transpose(first).astype(BF16)
            k1[:, at] = jnp.transpose(second).astype(BF16)
            v0[at, :] = jnp.where(low, value, 1.0).astype(BF16)
            v1[at, :] = jnp.where(low, 1.0, value).astype(BF16)

    end = length[0]

    def attend(size):
        lane = lax.broadcasted_iota(jnp.int32, (block, PAIR), 1)
        low = lane < HEAD
        both = q[...].astype(F32)
        q0 = jnp.where(low, both, jnp.where(lane == HEAD, 1.0, 0.0)).astype(BF16)
        q1 = jnp.where(low, jnp.where(lane == 0, 1.0, 0.0), both).astype(BF16)
        step = 512
        chunks = [slice(at, min(at + step, size)) for at in range(0, size, step)]
        lowest = jnp.full((block, PAIR), -3e38, F32)
        zero = jnp.zeros((block, PAIR), F32)

        def score(query, k, s, at, top):
            scores = jnp.dot(query, k[:, at], preferred_element_type=F32)
            s[:, at] = scores
            return jnp.maximum(top, lane_max(scores, at.stop - at.start))

        def mix(s, v, top, at, total):
            weights = jnp.exp2(s[:, at] - top).astype(BF16)
            return total + jnp.dot(weights, v[at, :], preferred_element_type=F32)

        top0, top1, t0, t1 = lowest, lowest, zero, zero
        for at in chunks:
            top0 = score(q0, k0, s0, at, top0)
        top0 = jnp.max(top0, axis=1, keepdims=True)
        for at in chunks:
            top1 = score(q1, k1, s1, at, top1)
            t0 = mix(s0, v0, top0, at, t0)
        top1 = jnp.max(top1, axis=1, keepdims=True)
        for at in chunks:
            t1 = mix(s1, v1, top1, at, t1)
        sums = pltpu.roll(jnp.where(low, t1, t0), HEAD, 1)
        out[...] = (jnp.where(low, t0, t1) / sums).astype(BF16)

    for below, size in zip((0, *SIZES[:-1]), SIZES):
        pl.when((end > below) & (end <= size))(functools.partial(attend, size))


def cross_attention(kv, q, block=256):
    rows = kv.shape[0]
    nodes = q.shape[0]
    return pl.pallas_call(
        cross_kernel,
        grid=(nodes // block,),
        out_shape=jax.ShapeDtypeStruct(q.shape, BF16),
        in_specs=[
            pl.BlockSpec((rows, 2 * PAIR), lambda j: (0, 0)),
            pl.BlockSpec((block, PAIR), lambda j: (j, 0)),
        ],
        out_specs=pl.BlockSpec((block, PAIR), lambda j: (j, 0)),
        scratch_shapes=[
            pltpu.VMEM((rows + SPARE, 2 * PAIR), BF16),
            pltpu.VMEM((PAIR, rows), BF16),
            pltpu.VMEM((PAIR, rows), BF16),
            pltpu.VMEM((rows, PAIR), BF16),
            pltpu.VMEM((rows, PAIR), BF16),
            pltpu.VMEM((block, rows), F32),
            pltpu.VMEM((block, rows), F32),
            pltpu.SMEM((1,), jnp.int32),
        ],
        compiler_params=params(),
        name="cross_attention",
    )(kv, q)


def window_kernel(block, edge, q, key_low, key_own, key_high, value_low, value_own, value_high, out, bias):
    nodes = q.shape[0]
    half = key_low.shape[0]
    wide = block + 2 * half
    first = edge[0]
    last = edge[1]

    @pl.when(pl.program_id(0) == 0)
    def _():
        row = lax.broadcasted_iota(jnp.int32, (block, wide), 0)
        column = lax.broadcasted_iota(jnp.int32, (block, wide), 1)
        near = (column >= row) & (column <= row + 2 * half)
        for b in range(nodes // block):
            there = (column + b * block >= first) & (column + b * block < last)
            bias[b] = jnp.where(near & there, 0.0, MASKED)

    keys = jnp.concatenate([key_low[...], key_own[...], key_high[...]], axis=0)
    values = jnp.concatenate([value_low[...], value_own[...], value_high[...]], axis=0).astype(F32)
    low_keys = lax.broadcasted_iota(jnp.int32, values.shape, 1) < HEAD
    v0 = jnp.where(low_keys, values, 1.0).astype(BF16)
    v1 = jnp.where(low_keys, 1.0, values).astype(BF16)
    low = lax.broadcasted_iota(jnp.int32, (block, PAIR), 1) < HEAD
    for b in range(nodes // block):
        both = q[b * block : (b + 1) * block, :].astype(F32)
        q0 = jnp.where(low, both, 0.0).astype(BF16)
        q1 = jnp.where(low, 0.0, both).astype(BF16)
        near = slice(b * block, b * block + wide)
        a0 = lax.dot_general(q0, keys[near], NT, preferred_element_type=F32) + bias[b]
        a1 = lax.dot_general(q1, keys[near], NT, preferred_element_type=F32) + bias[b]
        p0 = jnp.exp2(a0 - jnp.max(a0, axis=1, keepdims=True)).astype(BF16)
        p1 = jnp.exp2(a1 - jnp.max(a1, axis=1, keepdims=True)).astype(BF16)
        t0 = jnp.dot(p0, v0[near], preferred_element_type=F32)
        t1 = jnp.dot(p1, v1[near], preferred_element_type=F32)
        sums = pltpu.roll(jnp.where(low, t1, t0), HEAD, 1)
        out[b * block : (b + 1) * block, :] = (jnp.where(low, t0, t1) / sums).astype(BF16)


def window_attention(edge, proj, low, high, block=128):
    nodes = proj.shape[0]
    half = low.shape[0]
    pairs = GROUPS
    return pl.pallas_call(
        functools.partial(window_kernel, block),
        grid=(pairs,),
        out_shape=jax.ShapeDtypeStruct((nodes, pairs * PAIR), BF16),
        in_specs=[
            pl.BlockSpec(memory_space=pltpu.SMEM),
            pl.BlockSpec((nodes, PAIR), lambda j: (0, j)),
            pl.BlockSpec((half, PAIR), lambda j: (0, j)),
            pl.BlockSpec((nodes, PAIR), lambda j: (0, j + pairs)),
            pl.BlockSpec((half, PAIR), lambda j: (0, j)),
            pl.BlockSpec((half, PAIR), lambda j: (0, j + pairs)),
            pl.BlockSpec((nodes, PAIR), lambda j: (0, j + 2 * pairs)),
            pl.BlockSpec((half, PAIR), lambda j: (0, j + pairs)),
        ],
        out_specs=pl.BlockSpec((nodes, PAIR), lambda j: (0, j)),
        scratch_shapes=[pltpu.VMEM((nodes // block, block, block + 2 * half), F32)],
        compiler_params=params(),
        name="window_attention",
    )(edge, proj, low, proj, high, low, proj, high)


def tail_kernel(ctx, before, self_out, w_in, w_back, out, x, xn, total):
    j = pl.program_id(0)
    wide = w_in.shape[0] * w_in.shape[1]

    @pl.when(j == 0)
    def _():
        mixed = jnp.dot(ctx[...], self_out[...], preferred_element_type=F32)
        after = (before[...].astype(F32) + mixed).astype(BF16)
        x[...] = after
        xn[...] = rms_norm(after)

    first = w_in[...].reshape(wide, w_in.shape[2])
    second = w_back[...].reshape(wide, w_back.shape[2])
    hidden = lax.dot_general(xn[...], first, NT, preferred_element_type=F32)
    hidden = jax.nn.gelu(hidden, approximate=True).astype(BF16)
    part = jnp.dot(hidden, second, preferred_element_type=F32)

    @pl.when(j == 0)
    def _():
        total[...] = part

    @pl.when(j > 0)
    def _():
        total[...] += part

    @pl.when(j == pl.num_programs(0) - 1)
    def _():
        out[...] = (x[...].astype(F32) + total[...]).astype(BF16)


def tail(ctx, before, self_out, weights, steps=4):
    nodes, width = ctx.shape
    devices, _, units, _ = weights.shape
    return pl.pallas_call(
        tail_kernel,
        grid=(steps,),
        out_shape=jax.ShapeDtypeStruct(ctx.shape, BF16),
        in_specs=[
            pl.BlockSpec((nodes, width), lambda j: (0, 0)),
            pl.BlockSpec((nodes, width), lambda j: (0, 0)),
            pl.BlockSpec((width, width), lambda j: (0, 0)),
            pl.BlockSpec((devices // steps, None, units, width), lambda j: (j, 0, 0, 0)),
            pl.BlockSpec((devices // steps, None, units, width), lambda j: (j, 1, 0, 0)),
        ],
        out_specs=pl.BlockSpec((nodes, width), lambda j: (0, 0)),
        scratch_shapes=[
            pltpu.VMEM((nodes, width), BF16),
            pltpu.VMEM((nodes, width), BF16),
            pltpu.VMEM((nodes, width), F32),
        ],
        compiler_params=params(),
        name="tail",
    )(ctx, before, self_out, weights, weights)


def shards(
    latent,
    observations,
    counts,
    cross_query,
    cross_kv,
    cross_out,
    self_qkv,
    self_out,
    mlp_in,
    mlp_out,
):
    nodes, width = latent.shape
    weights = lax.all_gather(jnp.stack([mlp_in.T, mlp_out.T]), LOC_STREAM)
    kv, q = project(
        counts.reshape(-1), observations.reshape(-1, width), latent, cross_kv, cross_query
    )
    kv_here, q_here = exchange(kv.reshape(LOC * GROUPS, CAP, 2 * PAIR), q)
    ctx = cross_attention(
        kv_here.reshape(-1, 2 * PAIR), q_here.reshape(-1, PAIR)
    )
    ctx = give_back(ctx.reshape(GROUPS, nodes, PAIR))
    cross_ctx = jnp.transpose(ctx, (1, 0, 2)).reshape(nodes, width)
    after_cross = (
        latent.astype(F32) + jnp.dot(cross_ctx, cross_out, preferred_element_type=F32)
    ).astype(BF16)
    proj = jnp.dot(rms_norm(after_cross), self_qkv, preferred_element_type=F32)
    scale = jnp.where(lax.broadcasted_iota(jnp.int32, (1, 3 * width), 1) < width, QSCALE, 1.0)
    proj = (proj * scale).astype(BF16)
    half = WIN // 2
    me = lax.axis_index(LOC_STREAM)
    count = LOC * GROUPS
    up = [(i, i + 1) for i in range(count - 1)]
    down = [(i + 1, i) for i in range(count - 1)]
    low = lax.ppermute(proj[nodes - half :, width:], LOC_STREAM, up)
    high = lax.ppermute(proj[:half, width:], LOC_STREAM, down)
    edge = jnp.stack(
        [jnp.where(me == 0, half, 0), jnp.where(me == count - 1, half + nodes, nodes + WIN)]
    ).astype(jnp.int32)
    self_ctx = window_attention(edge, proj, low, high)
    return tail(self_ctx, after_cross, self_out, weights)


def solution(mesh):
    finer = Mesh(mesh.devices.reshape(LOC, 4, 2), LOC_STREAM)
    return jax.shard_map(
        shards,
        mesh=finer,
        in_specs=(
            P(LOC_STREAM, None),
            P(STREAM, "loc", None, None, None),
            P(STREAM, "loc", None),
            P(),
            P(),
            P(),
            P(),
            P(),
            P(None, LOC_STREAM),
            P(None, LOC_STREAM),
        ),
        out_specs=P(LOC_STREAM, None),
        check_vma=False,
    )
```

```python
import functools
import math

import jax
import jax.numpy as jnp
from jax import lax
from jax.experimental import pallas as pl
from jax.experimental.pallas import tpu as pltpu
from jax.sharding import Mesh
from jax.sharding import PartitionSpec as P

HEADS = 16
HEAD = 64
PAIR = 128
GROUPS = 8
WIN = 512
LOC = 16
CAP = 32
STREAM = ("s0", "s1")
LOC_STREAM = ("loc", "s0", "s1")
EPSILON = 1e-06
MASKED = -1e30
PADDING = 1e30
PADDING_FROM = 1e29
QSCALE = math.log2(math.e) / math.sqrt(HEAD)
MESH = pl.DeviceIdType.MESH
F32 = jnp.float32
BF16 = jnp.bfloat16
NT = (((1,), (1,)), ((), ()))
VMEM_LIMIT = 56 << 20


def params(**more):
    return pltpu.CompilerParams(vmem_limit_bytes=VMEM_LIMIT, **more)


def rms_norm(tensor):
    floats = tensor.astype(F32)
    return (floats * lax.rsqrt(jnp.mean(floats * floats, axis=-1, keepdims=True) + EPSILON)).astype(
        BF16
    )


def project_kernel(counts, obs, latent, wk, wv, wq, kv_out, q_out, xn, ln):
    @pl.when(pl.program_id(0) == 0)
    def _():
        xn[...] = rms_norm(obs[...])
        ln[...] = rms_norm(latent[...])

    q = (jnp.dot(ln[...], wq[...], preferred_element_type=F32) * QSCALE).astype(BF16)
    k = jnp.dot(xn[...], wk[...], preferred_element_type=F32)
    v = jnp.dot(xn[...], wv[...], preferred_element_type=F32)
    slot = lax.broadcasted_iota(jnp.int32, (CAP, PAIR), 0)
    for s in range(LOC):
        live = slot < counts[s]
        rows = slice(s * CAP, (s + 1) * CAP)
        for g in range(2):
            columns = slice(g * PAIR, (g + 1) * PAIR)
            kv_out[s, g, :, 0:PAIR] = jnp.where(live, k[rows, columns], PADDING).astype(BF16)
            kv_out[s, g, :, PAIR:] = jnp.where(live, v[rows, columns], PADDING).astype(BF16)
    for g in range(2):
        q_out[g] = q[:, g * PAIR : (g + 1) * PAIR]


def project(counts, obs, latent, cross_kv, cross_query):
    rows, width = obs.shape
    nodes = latent.shape[0]
    step = 2 * PAIR
    steps = width // step
    return pl.pallas_call(
        project_kernel,
        grid=(steps,),
        out_shape=(
            jax.ShapeDtypeStruct((LOC, GROUPS, CAP, 2 * PAIR), BF16),
            jax.ShapeDtypeStruct((GROUPS, nodes, PAIR), BF16),
        ),
        in_specs=[
            pl.BlockSpec(memory_space=pltpu.SMEM),
            pl.BlockSpec((rows, width), lambda j: (0, 0)),
            pl.BlockSpec((nodes, width), lambda j: (0, 0)),
            pl.BlockSpec((width, step), lambda j: (0, j)),
            pl.BlockSpec((width, step), lambda j: (0, j + steps)),
            pl.BlockSpec((width, step), lambda j: (0, j)),
        ],
        out_specs=(
            pl.BlockSpec((LOC, 2, CAP, 2 * PAIR), lambda j: (0, j, 0, 0)),
            pl.BlockSpec((2, nodes, PAIR), lambda j: (j, 0, 0)),
        ),
        scratch_shapes=[pltpu.VMEM((rows, width), BF16), pltpu.VMEM((nodes, width), BF16)],
        compiler_params=params(),
        name="project",
    )(counts, obs, latent, cross_kv, cross_kv, cross_query)


def exchange_kernel(kv, q, kv_here, q_here, kv_send, kv_recv, q_send, q_recv):
    loc = lax.axis_index("loc")
    me = lax.axis_index("s0") * 2 + lax.axis_index("s1")
    mine = loc * GROUPS + me
    pltpu.make_async_copy(q.at[me], q_here.at[me], q_recv).start()
    pltpu.make_async_copy(kv.at[mine], kv_here.at[me * LOC + loc], kv_recv).start()

    @pl.loop(1, GROUPS)
    def _(d):
        to = lax.rem(me + d, GROUPS)
        pltpu.make_async_remote_copy(
            q.at[to],
            q_here.at[me],
            q_send,
            q_recv,
            device_id=(loc, to // 2, lax.rem(to, 2)),
            device_id_type=MESH,
        ).start()

    @pl.loop(1, LOC * GROUPS)
    def _(d):
        to = lax.rem(mine + d, LOC * GROUPS)
        section = to // GROUPS
        group = lax.rem(to, GROUPS)
        pltpu.make_async_remote_copy(
            kv.at[to],
            kv_here.at[me * LOC + loc],
            kv_send,
            kv_recv,
            device_id=(section, group // 2, lax.rem(group, 2)),
            device_id_type=MESH,
        ).start()

    pltpu.make_async_copy(q.at[pl.ds(0, GROUPS - 1)], q_here.at[pl.ds(0, GROUPS - 1)], q_send).wait()
    pltpu.make_async_copy(q, q_here, q_recv).wait()

    sent = pl.ds(0, LOC * GROUPS - 1)
    pltpu.make_async_copy(kv.at[sent], kv_here.at[sent], kv_send).wait()
    pltpu.make_async_copy(kv_here, kv_here, kv_recv).wait()


def exchange(kv, q):
    return pl.pallas_call(
        exchange_kernel,
        out_shape=(
            jax.ShapeDtypeStruct(kv.shape, BF16),
            jax.ShapeDtypeStruct(q.shape, BF16),
        ),
        in_specs=[pl.BlockSpec(memory_space=pl.ANY)] * 2,
        out_specs=(pl.BlockSpec(memory_space=pl.ANY),) * 2,
        scratch_shapes=[pltpu.SemaphoreType.DMA] * 4,
        compiler_params=params(has_side_effects=True),
        name="exchange",
    )(kv, q)


def middle_kernel(
    latent, ctx, cross_out, self_qkv, after, q, kv,
    mixed, w_out, w_qkv, low, high, normed, w_sems, ctx_send, ctx_recv, send, recv,
):
    loc = lax.axis_index("loc")
    me = lax.axis_index("s0") * 2 + lax.axis_index("s1")
    flat = loc * GROUPS + me
    nodes, width = latent.shape
    half = low.shape[0]
    starts, ends = flat == 0, flat == LOC * GROUPS - 1
    outer_low = (me == 0) & jnp.logical_not(starts)
    outer_high = (me == GROUPS - 1) & jnp.logical_not(ends)

    def device(index):
        group = lax.rem(index, GROUPS)
        return index // GROUPS, group // 2, lax.rem(group, 2)

    load_out = pltpu.make_async_copy(cross_out, w_out, w_sems.at[0])
    load_qkv = pltpu.make_async_copy(self_qkv, w_qkv, w_sems.at[1])
    load_out.start()
    load_qkv.start()

    barrier = pltpu.get_barrier_semaphore()

    @pl.loop(1, GROUPS)
    def _(d):
        to = lax.rem(me + d, GROUPS)
        pl.semaphore_signal(
            barrier, inc=1, device_id=(loc, to // 2, lax.rem(to, 2)), device_id_type=MESH
        )

    @pl.when(outer_low)
    def _():
        pl.semaphore_signal(barrier, inc=1, device_id=device(flat - 1), device_id_type=MESH)

    @pl.when(outer_high)
    def _():
        pl.semaphore_signal(barrier, inc=1, device_id=device(flat + 1), device_id_type=MESH)

    pl.semaphore_wait(
        barrier, GROUPS - 1 + outer_low.astype(jnp.int32) + outer_high.astype(jnp.int32)
    )

    place = mixed.at[:, pl.ds(pl.multiple_of(me * PAIR, PAIR), PAIR)]

    @pl.loop(1, GROUPS)
    def _(d):
        to = lax.rem(me + d, GROUPS)
        pltpu.make_async_remote_copy(
            ctx.at[to],
            place,
            ctx_send,
            ctx_recv,
            device_id=(loc, to // 2, lax.rem(to, 2)),
            device_id_type=MESH,
        ).start()

    pltpu.make_async_copy(ctx.at[me], place, ctx_recv).start()

    @pl.when(starts)
    def _():
        low[...] = jnp.zeros_like(low)

    @pl.when(ends)
    def _():
        high[...] = jnp.zeros_like(high)

    load_out.wait()
    pltpu.make_async_copy(mixed, mixed, ctx_recv).wait()
    after[...] = (
        latent[...].astype(F32) + jnp.dot(mixed[...], w_out[...], preferred_element_type=F32)
    ).astype(BF16)

    down = pltpu.make_async_remote_copy(
        after.at[0:half], high, send.at[0], recv.at[1],
        device_id=device(jnp.maximum(flat - 1, 0)), device_id_type=MESH,
    )
    up = pltpu.make_async_remote_copy(
        after.at[nodes - half : nodes], low, send.at[1], recv.at[0],
        device_id=device(jnp.minimum(flat + 1, LOC * GROUPS - 1)), device_id_type=MESH,
    )
    pl.when(jnp.logical_not(starts))(down.start)
    pl.when(jnp.logical_not(ends))(up.start)

    normed[...] = rms_norm(after[...])
    load_qkv.wait()
    step = 512

    @pl.loop(0, width // step)
    def _(c):
        at = pl.ds(pl.multiple_of(c * step, step), step)
        found = jnp.dot(normed[...], w_qkv[:, at], preferred_element_type=F32)
        q[:, at] = (found * QSCALE).astype(BF16)

    def project(rows, to):
        @pl.loop(0, 2 * width // step)
        def _(c):
            at = pl.ds(pl.multiple_of(c * step, step), step)
            weights = w_qkv[:, pl.ds(pl.multiple_of(width + c * step, step), step)]
            kv[to, at] = jnp.dot(rows[...], weights, preferred_element_type=F32).astype(BF16)

    project(normed, slice(half, half + nodes))

    @pl.when(jnp.logical_not(starts))
    def _():
        pltpu.make_async_copy(low, low, recv.at[0]).wait()

    normed[0:half] = rms_norm(low[...])
    project(normed.at[0:half], slice(0, half))

    @pl.when(jnp.logical_not(ends))
    def _():
        pltpu.make_async_copy(high, high, recv.at[1]).wait()

    normed[0:half] = rms_norm(high[...])
    project(normed.at[0:half], slice(half + nodes, 2 * half + nodes))

    pl.when(jnp.logical_not(starts))(down.wait_send)
    pl.when(jnp.logical_not(ends))(up.wait_send)
    sent = ctx.at[pl.ds(0, GROUPS - 1)]
    pltpu.make_async_copy(sent, sent, ctx_send).wait()


def middle(latent, ctx, cross_out, self_qkv):
    nodes, width = latent.shape
    half = WIN // 2
    vmem = pl.BlockSpec(memory_space=pltpu.VMEM)
    away = pl.BlockSpec(memory_space=pl.ANY)
    return pl.pallas_call(
        middle_kernel,
        out_shape=(
            jax.ShapeDtypeStruct((nodes, width), BF16),
            jax.ShapeDtypeStruct((nodes, width), BF16),
            jax.ShapeDtypeStruct((nodes + WIN, 2 * width), BF16),
        ),
        in_specs=[vmem, away, away, away],
        out_specs=(vmem, vmem, vmem),
        scratch_shapes=[
            pltpu.VMEM((nodes, width), BF16),
            pltpu.VMEM((width, width), BF16),
            pltpu.VMEM((width, 3 * width), BF16),
            pltpu.VMEM((half, width), BF16),
            pltpu.VMEM((half, width), BF16),
            pltpu.VMEM((nodes, width), BF16),
            pltpu.SemaphoreType.DMA((2,)),
            pltpu.SemaphoreType.DMA,
            pltpu.SemaphoreType.DMA,
            pltpu.SemaphoreType.DMA((2,)),
            pltpu.SemaphoreType.DMA((2,)),
        ],
        compiler_params=params(has_side_effects=True, collective_id=1),
        name="middle",
    )(latent, ctx, cross_out, self_qkv)


PACK = 512
SIZES = (1024, 1536, 1792, 2048, 2304, 2560, 2816, 3072, 3584, 4096)
SPARE = 1024


def lane_max(scores, width):
    top = scores[:, 0:PAIR]
    for c in range(1, width // PAIR):
        top = jnp.maximum(top, scores[:, c * PAIR : (c + 1) * PAIR])
    return top


def pack_rows(kv, packed):
    row = lax.broadcasted_iota(jnp.int32, (PACK, PACK), 0)
    column = lax.broadcasted_iota(jnp.int32, (PACK, PACK), 1)
    slot = lax.broadcasted_iota(jnp.int32, (PACK, 2 * PAIR), 0)
    ones = jnp.ones((8, PACK), BF16)
    end = 0
    for g in range(kv.shape[0] // PACK):
        rows = kv[g * PACK : (g + 1) * PACK, :]
        live = rows[:, 0:1].astype(F32) < PADDING_FROM
        number = jnp.sum(live.astype(F32)).astype(jnp.int32)
        before = jnp.dot(ones, (live & (row < column)).astype(BF16), preferred_element_type=F32)
        itself = jnp.dot(ones, (live & (row == column)).astype(BF16), preferred_element_type=F32)
        place = jnp.where(itself > 0.5, before, -1.0)[0:1, :].astype(jnp.int32)
        pick = (place == row).astype(BF16)
        found = jnp.dot(pick, rows, preferred_element_type=F32)
        packed[pl.ds(pl.multiple_of(end, 16), PACK), :] = jnp.where(
            slot < number, found, PADDING
        ).astype(BF16)
        end = end + (number + 15) // 16 * 16
    packed[pl.ds(pl.multiple_of(end, 16), SPARE), :] = jnp.full((SPARE, 2 * PAIR), PADDING, BF16)
    return end


def cross_kernel(kv, q, out, packed, k0, k1, v0, v1, s0, s1, length):
    block = q.shape[0]

    @pl.when(pl.program_id(0) == 0)
    def _():
        end = pack_rows(kv, packed)
        length[0] = end
        lane = lax.broadcasted_iota(jnp.int32, (PACK, PAIR), 1)
        low = lane < HEAD

        @pl.loop(0, jnp.maximum((end + PACK - 1) // PACK, SIZES[0] // PACK))
        def _(b):
            at = pl.ds(pl.multiple_of(b * PACK, PACK), PACK)
            key = packed[at, 0:PAIR].astype(F32)
            value = packed[at, PAIR:].astype(F32)
            live = key < PADDING_FROM
            bias = jnp.where(live, 0.0, MASKED)
            key = jnp.where(live, key, 0.0)
            value = jnp.where(live, value, 0.0)
            first = jnp.where(low, key, jnp.where(lane == HEAD, bias, 0.0))
            second = jnp.where(low, jnp.where(lane == 0, bias, 0.0), key)
            k0[:, at] = jnp.transpose(first).astype(BF16)
            k1[:, at] = jnp.transpose(second).astype(BF16)
            v0[at, :] = jnp.where(low, value, 1.0).astype(BF16)
            v1[at, :] = jnp.where(low, 1.0, value).astype(BF16)

    end = length[0]

    def attend(size):
        lane = lax.broadcasted_iota(jnp.int32, (block, PAIR), 1)
        low = lane < HEAD
        both = q[...].astype(F32)
        q0 = jnp.where(low, both, jnp.where(lane == HEAD, 1.0, 0.0)).astype(BF16)
        q1 = jnp.where(low, jnp.where(lane == 0, 1.0, 0.0), both).astype(BF16)
        step = 512
        chunks = [slice(at, min(at + step, size)) for at in range(0, size, step)]
        lowest = jnp.full((block, PAIR), -3e38, F32)
        zero = jnp.zeros((block, PAIR), F32)

        def score(query, k, s, at, top):
            scores = jnp.dot(query, k[:, at], preferred_element_type=F32)
            s[:, at] = scores
            return jnp.maximum(top, lane_max(scores, at.stop - at.start))

        def mix(s, v, top, at, total):
            weights = jnp.exp2(s[:, at] - top).astype(BF16)
            return total + jnp.dot(weights, v[at, :], preferred_element_type=F32)

        top0, top1, t0, t1 = lowest, lowest, zero, zero
        for at in chunks:
            top0 = score(q0, k0, s0, at, top0)
        top0 = jnp.max(top0, axis=1, keepdims=True)
        for at in chunks:
            top1 = score(q1, k1, s1, at, top1)
            t0 = mix(s0, v0, top0, at, t0)
        top1 = jnp.max(top1, axis=1, keepdims=True)
        for at in chunks:
            t1 = mix(s1, v1, top1, at, t1)
        sums = pltpu.roll(jnp.where(low, t1, t0), HEAD, 1)
        out[...] = (jnp.where(low, t0, t1) / sums).astype(BF16)

    for below, size in zip((0, *SIZES[:-1]), SIZES):
        pl.when((end > below) & (end <= size))(functools.partial(attend, size))


def cross_attention(kv, q, block=256):
    rows = kv.shape[0]
    nodes = q.shape[0]
    return pl.pallas_call(
        cross_kernel,
        grid=(nodes // block,),
        out_shape=jax.ShapeDtypeStruct(q.shape, BF16),
        in_specs=[
            pl.BlockSpec((rows, 2 * PAIR), lambda j: (0, 0)),
            pl.BlockSpec((block, PAIR), lambda j: (j, 0)),
        ],
        out_specs=pl.BlockSpec((block, PAIR), lambda j: (j, 0)),
        scratch_shapes=[
            pltpu.VMEM((rows + SPARE, 2 * PAIR), BF16),
            pltpu.VMEM((PAIR, rows), BF16),
            pltpu.VMEM((PAIR, rows), BF16),
            pltpu.VMEM((rows, PAIR), BF16),
            pltpu.VMEM((rows, PAIR), BF16),
            pltpu.VMEM((block, rows), F32),
            pltpu.VMEM((block, rows), F32),
            pltpu.SMEM((1,), jnp.int32),
        ],
        compiler_params=params(),
        name="cross_attention",
    )(kv, q)


def window_kernel(block, q, key, value, out, bias):
    nodes = q.shape[0]
    window = key.shape[0]
    half = (window - nodes) // 2
    wide = block + 2 * half
    me = (lax.axis_index("loc") * 4 + lax.axis_index("s0")) * 2 + lax.axis_index("s1")

    @pl.when(pl.program_id(0) == 0)
    def _():
        first = jnp.where(me == 0, half, 0)
        last = jnp.where(me == LOC * GROUPS - 1, half + nodes, window)
        row = lax.broadcasted_iota(jnp.int32, (block, wide), 0)
        column = lax.broadcasted_iota(jnp.int32, (block, wide), 1)
        near = (column >= row) & (column <= row + 2 * half)
        for b in range(nodes // block):
            there = (column + b * block >= first) & (column + b * block < last)
            bias[b] = jnp.where(near & there, 0.0, MASKED)

    values = value[...].astype(F32)
    low_values = lax.broadcasted_iota(jnp.int32, values.shape, 1) < HEAD
    v0 = jnp.where(low_values, values, 1.0).astype(BF16)
    v1 = jnp.where(low_values, 1.0, values).astype(BF16)
    low = lax.broadcasted_iota(jnp.int32, (block, PAIR), 1) < HEAD
    for b in range(nodes // block):
        both = q[b * block : (b + 1) * block, :].astype(F32)
        q0 = jnp.where(low, both, 0.0).astype(BF16)
        q1 = jnp.where(low, 0.0, both).astype(BF16)
        near = slice(b * block, b * block + wide)
        a0 = lax.dot_general(q0, key[near, :], NT, preferred_element_type=F32) + bias[b]
        a1 = lax.dot_general(q1, key[near, :], NT, preferred_element_type=F32) + bias[b]
        p0 = jnp.exp2(a0 - jnp.max(a0, axis=1, keepdims=True)).astype(BF16)
        p1 = jnp.exp2(a1 - jnp.max(a1, axis=1, keepdims=True)).astype(BF16)
        t0 = jnp.dot(p0, v0[near], preferred_element_type=F32)
        t1 = jnp.dot(p1, v1[near], preferred_element_type=F32)
        sums = pltpu.roll(jnp.where(low, t1, t0), HEAD, 1)
        out[b * block : (b + 1) * block, :] = (jnp.where(low, t0, t1) / sums).astype(BF16)


def window_attention(q, kv, block=128):
    nodes = q.shape[0]
    window = kv.shape[0]
    return pl.pallas_call(
        functools.partial(window_kernel, block),
        grid=(GROUPS,),
        out_shape=jax.ShapeDtypeStruct(q.shape, BF16),
        in_specs=[
            pl.BlockSpec((nodes, PAIR), lambda j: (0, j)),
            pl.BlockSpec((window, PAIR), lambda j: (0, j)),
            pl.BlockSpec((window, PAIR), lambda j: (0, j + GROUPS)),
        ],
        out_specs=pl.BlockSpec((nodes, PAIR), lambda j: (0, j)),
        scratch_shapes=[pltpu.VMEM((nodes // block, block, block + window - nodes), F32)],
        compiler_params=params(),
        name="window_attention",
    )(q, kv, kv)


def tail_kernel(ctx, before, self_out, w_in, w_back, out, x, xn, total):
    j = pl.program_id(0)
    wide = w_in.shape[0] * w_in.shape[1]

    @pl.when(j == 0)
    def _():
        mixed = jnp.dot(ctx[...], self_out[...], preferred_element_type=F32)
        after = (before[...].astype(F32) + mixed).astype(BF16)
        x[...] = after
        xn[...] = rms_norm(after)

    first = w_in[...].reshape(wide, w_in.shape[2])
    second = w_back[...].reshape(wide, w_back.shape[2])
    hidden = lax.dot_general(xn[...], first, NT, preferred_element_type=F32)
    hidden = jax.nn.gelu(hidden, approximate=True).astype(BF16)
    part = jnp.dot(hidden, second, preferred_element_type=F32)

    @pl.when(j == 0)
    def _():
        total[...] = part

    @pl.when(j > 0)
    def _():
        total[...] += part

    @pl.when(j == pl.num_programs(0) - 1)
    def _():
        out[...] = (x[...].astype(F32) + total[...]).astype(BF16)


def tail(ctx, before, self_out, weights, steps=4):
    nodes, width = ctx.shape
    devices, _, units, _ = weights.shape
    return pl.pallas_call(
        tail_kernel,
        grid=(steps,),
        out_shape=jax.ShapeDtypeStruct(ctx.shape, BF16),
        in_specs=[
            pl.BlockSpec((nodes, width), lambda j: (0, 0)),
            pl.BlockSpec((nodes, width), lambda j: (0, 0)),
            pl.BlockSpec((width, width), lambda j: (0, 0)),
            pl.BlockSpec((devices // steps, None, units, width), lambda j: (j, 0, 0, 0)),
            pl.BlockSpec((devices // steps, None, units, width), lambda j: (j, 1, 0, 0)),
        ],
        out_specs=pl.BlockSpec((nodes, width), lambda j: (0, 0)),
        scratch_shapes=[
            pltpu.VMEM((nodes, width), BF16),
            pltpu.VMEM((nodes, width), BF16),
            pltpu.VMEM((nodes, width), F32),
        ],
        compiler_params=params(),
        name="tail",
    )(ctx, before, self_out, weights, weights)


def shards(
    latent,
    observations,
    counts,
    cross_query,
    cross_kv,
    cross_out,
    self_qkv,
    self_out,
    mlp_in,
    mlp_out,
):
    nodes, width = latent.shape
    weights = lax.all_gather(jnp.stack([mlp_in.T, mlp_out.T]), LOC_STREAM)
    kv, q = project(
        counts.reshape(-1), observations.reshape(-1, width), latent, cross_kv, cross_query
    )
    kv_here, q_here = exchange(kv.reshape(LOC * GROUPS, CAP, 2 * PAIR), q)
    ctx = cross_attention(
        kv_here.reshape(-1, 2 * PAIR), q_here.reshape(-1, PAIR)
    )
    after_cross, self_q, self_kv = middle(
        latent, ctx.reshape(GROUPS, nodes, PAIR), cross_out, self_qkv
    )
    self_ctx = window_attention(self_q, self_kv)
    return tail(self_ctx, after_cross, self_out, weights)


def solution(mesh):
    finer = Mesh(mesh.devices.reshape(LOC, 4, 2), LOC_STREAM)
    return jax.shard_map(
        shards,
        mesh=finer,
        in_specs=(
            P(LOC_STREAM, None),
            P(STREAM, "loc", None, None, None),
            P(STREAM, "loc", None),
            P(),
            P(),
            P(),
            P(),
            P(),
            P(None, LOC_STREAM),
            P(None, LOC_STREAM),
        ),
        out_specs=P(LOC_STREAM, None),
        check_vma=False,
    )
```

```python
import functools
import math

import jax
import jax.numpy as jnp
from jax import lax
from jax.experimental import pallas as pl
from jax.experimental.pallas import tpu as pltpu
from jax.sharding import Mesh
from jax.sharding import PartitionSpec as P

HEADS = 16
HEAD = 64
PAIR = 128
GROUPS = 8
WIN = 512
LOC = 16
CAP = 32
STREAM = ("s0", "s1")
LOC_STREAM = ("loc", "s0", "s1")
EPSILON = 1e-06
MASKED = -1e30
PADDING = 1e30
PADDING_FROM = 1e29
QSCALE = math.log2(math.e) / math.sqrt(HEAD)
MESH = pl.DeviceIdType.MESH
F32 = jnp.float32
BF16 = jnp.bfloat16
NT = (((1,), (1,)), ((), ()))
VMEM_LIMIT = 56 << 20


def params(**more):
    return pltpu.CompilerParams(vmem_limit_bytes=VMEM_LIMIT, **more)


def rms_norm(tensor):
    floats = tensor.astype(F32)
    return (floats * lax.rsqrt(jnp.mean(floats * floats, axis=-1, keepdims=True) + EPSILON)).astype(
        BF16
    )


def project_kernel(
    counts, obs, latent, wk, wv, wq, w_in, w_back, kv_out, q_out, column,
    xn, ln, send, recv,
):
    loc = lax.axis_index("loc")
    z = lax.axis_index("s0")
    core = lax.axis_index("s1")
    step = pl.program_id(0)

    @pl.when(step == 0)
    def _():
        barrier = pltpu.get_barrier_semaphore()
        for d in range(1, 4):
            pl.semaphore_signal(
                barrier, inc=1, device_id=(loc, lax.rem(z + d, 4), core), device_id_type=MESH
            )
        xn[...] = rms_norm(obs[...])
        ln[...] = rms_norm(latent[...])

    @pl.when(step == 1)
    def _():
        pl.semaphore_wait(pltpu.get_barrier_semaphore(), 3)
        for at, part in enumerate((w_in, w_back)):
            pltpu.make_async_copy(part, column.at[z, at], recv).start()
            for d in range(1, 4):
                pltpu.make_async_remote_copy(
                    part, column.at[z, at], send, recv,
                    device_id=(loc, lax.rem(z + d, 4), core), device_id_type=MESH,
                ).start()

    q = (jnp.dot(ln[...], wq[...], preferred_element_type=F32) * QSCALE).astype(BF16)
    k = jnp.dot(xn[...], wk[...], preferred_element_type=F32)
    v = jnp.dot(xn[...], wv[...], preferred_element_type=F32)
    slot = lax.broadcasted_iota(jnp.int32, (CAP, PAIR), 0)
    for s in range(LOC):
        live = slot < counts[s]
        rows = slice(s * CAP, (s + 1) * CAP)
        for g in range(2):
            columns = slice(g * PAIR, (g + 1) * PAIR)
            kv_out[s, g, :, 0:PAIR] = jnp.where(live, k[rows, columns], PADDING).astype(BF16)
            kv_out[s, g, :, PAIR:] = jnp.where(live, v[rows, columns], PADDING).astype(BF16)
    for g in range(2):
        q_out[g] = q[:, g * PAIR : (g + 1) * PAIR]

    @pl.when(step == pl.num_programs(0) - 1)
    def _():
        sent = column.at[pl.ds(0, 3)]
        pltpu.make_async_copy(sent, sent, send).wait()
        pltpu.make_async_copy(column, column, recv).wait()


def project(counts, obs, latent, cross_kv, cross_query, w_in, w_back):
    rows, width = obs.shape
    nodes = latent.shape[0]
    step = 2 * PAIR
    steps = width // step
    return pl.pallas_call(
        project_kernel,
        grid=(steps,),
        out_shape=(
            jax.ShapeDtypeStruct((LOC, GROUPS, CAP, 2 * PAIR), BF16),
            jax.ShapeDtypeStruct((GROUPS, nodes, PAIR), BF16),
            jax.ShapeDtypeStruct((4, 2, *w_in.shape), BF16),
        ),
        in_specs=[
            pl.BlockSpec(memory_space=pltpu.SMEM),
            pl.BlockSpec((rows, width), lambda j: (0, 0)),
            pl.BlockSpec((nodes, width), lambda j: (0, 0)),
            pl.BlockSpec((width, step), lambda j: (0, j)),
            pl.BlockSpec((width, step), lambda j: (0, j + steps)),
            pl.BlockSpec((width, step), lambda j: (0, j)),
            pl.BlockSpec(memory_space=pl.ANY),
            pl.BlockSpec(memory_space=pl.ANY),
        ],
        out_specs=(
            pl.BlockSpec((LOC, 2, CAP, 2 * PAIR), lambda j: (0, j, 0, 0)),
            pl.BlockSpec((2, nodes, PAIR), lambda j: (j, 0, 0)),
            pl.BlockSpec(memory_space=pl.ANY),
        ),
        scratch_shapes=[
            pltpu.VMEM((rows, width), BF16),
            pltpu.VMEM((nodes, width), BF16),
            pltpu.SemaphoreType.DMA,
            pltpu.SemaphoreType.DMA,
        ],
        compiler_params=params(has_side_effects=True, collective_id=2),
        name="project",
    )(counts, obs, latent, cross_kv, cross_kv, cross_query, w_in, w_back)


def exchange_kernel(kv, q, kv_here, q_here, kv_send, kv_recv, q_send, q_recv):
    loc = lax.axis_index("loc")
    me = lax.axis_index("s0") * 2 + lax.axis_index("s1")
    mine = loc * GROUPS + me
    pltpu.make_async_copy(q.at[me], q_here.at[me], q_recv).start()
    pltpu.make_async_copy(kv.at[mine], kv_here.at[me * LOC + loc], kv_recv).start()

    @pl.loop(1, GROUPS)
    def _(d):
        to = lax.rem(me + d, GROUPS)
        pltpu.make_async_remote_copy(
            q.at[to],
            q_here.at[me],
            q_send,
            q_recv,
            device_id=(loc, to // 2, lax.rem(to, 2)),
            device_id_type=MESH,
        ).start()

    @pl.loop(1, LOC * GROUPS)
    def _(d):
        to = lax.rem(mine + d, LOC * GROUPS)
        section = to // GROUPS
        group = lax.rem(to, GROUPS)
        pltpu.make_async_remote_copy(
            kv.at[to],
            kv_here.at[me * LOC + loc],
            kv_send,
            kv_recv,
            device_id=(section, group // 2, lax.rem(group, 2)),
            device_id_type=MESH,
        ).start()

    pltpu.make_async_copy(q.at[pl.ds(0, GROUPS - 1)], q_here.at[pl.ds(0, GROUPS - 1)], q_send).wait()
    pltpu.make_async_copy(q, q_here, q_recv).wait()

    sent = pl.ds(0, LOC * GROUPS - 1)
    pltpu.make_async_copy(kv.at[sent], kv_here.at[sent], kv_send).wait()
    pltpu.make_async_copy(kv_here, kv_here, kv_recv).wait()


def exchange(kv, q):
    return pl.pallas_call(
        exchange_kernel,
        out_shape=(
            jax.ShapeDtypeStruct(kv.shape, BF16),
            jax.ShapeDtypeStruct(q.shape, BF16),
        ),
        in_specs=[pl.BlockSpec(memory_space=pl.ANY)] * 2,
        out_specs=(pl.BlockSpec(memory_space=pl.ANY),) * 2,
        scratch_shapes=[pltpu.SemaphoreType.DMA] * 4,
        compiler_params=params(has_side_effects=True),
        name="exchange",
    )(kv, q)


def middle_kernel(
    latent, ctx, cross_out, self_qkv, after, q, kv,
    mixed, w_out, w_qkv, low, high, normed, w_sems, ctx_send, ctx_recv, send, recv,
):
    loc = lax.axis_index("loc")
    me = lax.axis_index("s0") * 2 + lax.axis_index("s1")
    flat = loc * GROUPS + me
    nodes, width = latent.shape
    half = low.shape[0]
    starts, ends = flat == 0, flat == LOC * GROUPS - 1
    outer_low = (me == 0) & jnp.logical_not(starts)
    outer_high = (me == GROUPS - 1) & jnp.logical_not(ends)

    def device(index):
        group = lax.rem(index, GROUPS)
        return index // GROUPS, group // 2, lax.rem(group, 2)

    load_out = pltpu.make_async_copy(cross_out, w_out, w_sems.at[0])
    load_qkv = pltpu.make_async_copy(self_qkv, w_qkv, w_sems.at[1])
    load_out.start()
    load_qkv.start()

    barrier = pltpu.get_barrier_semaphore()

    @pl.loop(1, GROUPS)
    def _(d):
        to = lax.rem(me + d, GROUPS)
        pl.semaphore_signal(
            barrier, inc=1, device_id=(loc, to // 2, lax.rem(to, 2)), device_id_type=MESH
        )

    @pl.when(outer_low)
    def _():
        pl.semaphore_signal(barrier, inc=1, device_id=device(flat - 1), device_id_type=MESH)

    @pl.when(outer_high)
    def _():
        pl.semaphore_signal(barrier, inc=1, device_id=device(flat + 1), device_id_type=MESH)

    pl.semaphore_wait(
        barrier, GROUPS - 1 + outer_low.astype(jnp.int32) + outer_high.astype(jnp.int32)
    )

    place = mixed.at[:, pl.ds(pl.multiple_of(me * PAIR, PAIR), PAIR)]

    @pl.loop(1, GROUPS)
    def _(d):
        to = lax.rem(me + d, GROUPS)
        pltpu.make_async_remote_copy(
            ctx.at[to],
            place,
            ctx_send,
            ctx_recv,
            device_id=(loc, to // 2, lax.rem(to, 2)),
            device_id_type=MESH,
        ).start()

    pltpu.make_async_copy(ctx.at[me], place, ctx_recv).start()

    @pl.when(starts)
    def _():
        low[...] = jnp.zeros_like(low)

    @pl.when(ends)
    def _():
        high[...] = jnp.zeros_like(high)

    load_out.wait()
    pltpu.make_async_copy(mixed, mixed, ctx_recv).wait()
    after[...] = (
        latent[...].astype(F32) + jnp.dot(mixed[...], w_out[...], preferred_element_type=F32)
    ).astype(BF16)

    down = pltpu.make_async_remote_copy(
        after.at[0:half], high, send.at[0], recv.at[1],
        device_id=device(jnp.maximum(flat - 1, 0)), device_id_type=MESH,
    )
    up = pltpu.make_async_remote_copy(
        after.at[nodes - half : nodes], low, send.at[1], recv.at[0],
        device_id=device(jnp.minimum(flat + 1, LOC * GROUPS - 1)), device_id_type=MESH,
    )
    pl.when(jnp.logical_not(starts))(down.start)
    pl.when(jnp.logical_not(ends))(up.start)

    normed[...] = rms_norm(after[...])
    load_qkv.wait()
    step = 512

    @pl.loop(0, width // step)
    def _(c):
        at = pl.ds(pl.multiple_of(c * step, step), step)
        found = jnp.dot(normed[...], w_qkv[:, at], preferred_element_type=F32)
        q[:, at] = (found * QSCALE).astype(BF16)

    def project(rows, to):
        @pl.loop(0, 2 * width // step)
        def _(c):
            at = pl.ds(pl.multiple_of(c * step, step), step)
            weights = w_qkv[:, pl.ds(pl.multiple_of(width + c * step, step), step)]
            kv[to, at] = jnp.dot(rows[...], weights, preferred_element_type=F32).astype(BF16)

    project(normed, slice(half, half + nodes))

    @pl.when(jnp.logical_not(starts))
    def _():
        pltpu.make_async_copy(low, low, recv.at[0]).wait()

    normed[0:half] = rms_norm(low[...])
    project(normed.at[0:half], slice(0, half))

    @pl.when(jnp.logical_not(ends))
    def _():
        pltpu.make_async_copy(high, high, recv.at[1]).wait()

    normed[0:half] = rms_norm(high[...])
    project(normed.at[0:half], slice(half + nodes, 2 * half + nodes))

    pl.when(jnp.logical_not(starts))(down.wait_send)
    pl.when(jnp.logical_not(ends))(up.wait_send)
    sent = ctx.at[pl.ds(0, GROUPS - 1)]
    pltpu.make_async_copy(sent, sent, ctx_send).wait()


def middle(latent, ctx, cross_out, self_qkv):
    nodes, width = latent.shape
    half = WIN // 2
    vmem = pl.BlockSpec(memory_space=pltpu.VMEM)
    away = pl.BlockSpec(memory_space=pl.ANY)
    return pl.pallas_call(
        middle_kernel,
        out_shape=(
            jax.ShapeDtypeStruct((nodes, width), BF16),
            jax.ShapeDtypeStruct((nodes, width), BF16),
            jax.ShapeDtypeStruct((nodes + WIN, 2 * width), BF16),
        ),
        in_specs=[vmem, away, away, away],
        out_specs=(vmem, vmem, vmem),
        scratch_shapes=[
            pltpu.VMEM((nodes, width), BF16),
            pltpu.VMEM((width, width), BF16),
            pltpu.VMEM((width, 3 * width), BF16),
            pltpu.VMEM((half, width), BF16),
            pltpu.VMEM((half, width), BF16),
            pltpu.VMEM((nodes, width), BF16),
            pltpu.SemaphoreType.DMA((2,)),
            pltpu.SemaphoreType.DMA,
            pltpu.SemaphoreType.DMA,
            pltpu.SemaphoreType.DMA((2,)),
            pltpu.SemaphoreType.DMA((2,)),
        ],
        compiler_params=params(has_side_effects=True, collective_id=1),
        name="middle",
    )(latent, ctx, cross_out, self_qkv)


PACK = 512
SIZES = (1024, 1536, 1792, 2048, 2304, 2560, 2816, 3072, 3584, 4096)
SPARE = 1024


def lane_max(scores, width):
    top = scores[:, 0:PAIR]
    for c in range(1, width // PAIR):
        top = jnp.maximum(top, scores[:, c * PAIR : (c + 1) * PAIR])
    return top


def pack_rows(kv, packed):
    row = lax.broadcasted_iota(jnp.int32, (PACK, PACK), 0)
    column = lax.broadcasted_iota(jnp.int32, (PACK, PACK), 1)
    slot = lax.broadcasted_iota(jnp.int32, (PACK, 2 * PAIR), 0)
    ones = jnp.ones((8, PACK), BF16)
    end = 0
    for g in range(kv.shape[0] // PACK):
        rows = kv[g * PACK : (g + 1) * PACK, :]
        live = rows[:, 0:1].astype(F32) < PADDING_FROM
        number = jnp.sum(live.astype(F32)).astype(jnp.int32)
        before = jnp.dot(ones, (live & (row < column)).astype(BF16), preferred_element_type=F32)
        itself = jnp.dot(ones, (live & (row == column)).astype(BF16), preferred_element_type=F32)
        place = jnp.where(itself > 0.5, before, -1.0)[0:1, :].astype(jnp.int32)
        pick = (place == row).astype(BF16)
        found = jnp.dot(pick, rows, preferred_element_type=F32)
        packed[pl.ds(pl.multiple_of(end, 16), PACK), :] = jnp.where(
            slot < number, found, PADDING
        ).astype(BF16)
        end = end + (number + 15) // 16 * 16
    packed[pl.ds(pl.multiple_of(end, 16), SPARE), :] = jnp.full((SPARE, 2 * PAIR), PADDING, BF16)
    return end


def cross_kernel(kv, q, out, packed, k0, k1, v0, v1, s0, s1, length):
    block = q.shape[0]

    @pl.when(pl.program_id(0) == 0)
    def _():
        end = pack_rows(kv, packed)
        length[0] = end
        lane = lax.broadcasted_iota(jnp.int32, (PACK, PAIR), 1)
        low = lane < HEAD

        @pl.loop(0, jnp.maximum((end + PACK - 1) // PACK, SIZES[0] // PACK))
        def _(b):
            at = pl.ds(pl.multiple_of(b * PACK, PACK), PACK)
            key = packed[at, 0:PAIR].astype(F32)
            value = packed[at, PAIR:].astype(F32)
            live = key < PADDING_FROM
            bias = jnp.where(live, 0.0, MASKED)
            key = jnp.where(live, key, 0.0)
            value = jnp.where(live, value, 0.0)
            first = jnp.where(low, key, jnp.where(lane == HEAD, bias, 0.0))
            second = jnp.where(low, jnp.where(lane == 0, bias, 0.0), key)
            k0[:, at] = jnp.transpose(first).astype(BF16)
            k1[:, at] = jnp.transpose(second).astype(BF16)
            v0[at, :] = jnp.where(low, value, 1.0).astype(BF16)
            v1[at, :] = jnp.where(low, 1.0, value).astype(BF16)

    end = length[0]

    def attend(size):
        lane = lax.broadcasted_iota(jnp.int32, (block, PAIR), 1)
        low = lane < HEAD
        both = q[...].astype(F32)
        q0 = jnp.where(low, both, jnp.where(lane == HEAD, 1.0, 0.0)).astype(BF16)
        q1 = jnp.where(low, jnp.where(lane == 0, 1.0, 0.0), both).astype(BF16)
        step = 512
        chunks = [slice(at, min(at + step, size)) for at in range(0, size, step)]
        lowest = jnp.full((block, PAIR), -3e38, F32)
        zero = jnp.zeros((block, PAIR), F32)

        def score(query, k, s, at, top):
            scores = jnp.dot(query, k[:, at], preferred_element_type=F32)
            s[:, at] = scores
            return jnp.maximum(top, lane_max(scores, at.stop - at.start))

        def mix(s, v, top, at, total):
            weights = jnp.exp2(s[:, at] - top).astype(BF16)
            return total + jnp.dot(weights, v[at, :], preferred_element_type=F32)

        top0, top1, t0, t1 = lowest, lowest, zero, zero
        for at in chunks:
            top0 = score(q0, k0, s0, at, top0)
        top0 = jnp.max(top0, axis=1, keepdims=True)
        for at in chunks:
            top1 = score(q1, k1, s1, at, top1)
            t0 = mix(s0, v0, top0, at, t0)
        top1 = jnp.max(top1, axis=1, keepdims=True)
        for at in chunks:
            t1 = mix(s1, v1, top1, at, t1)
        sums = pltpu.roll(jnp.where(low, t1, t0), HEAD, 1)
        out[...] = (jnp.where(low, t0, t1) / sums).astype(BF16)

    for below, size in zip((0, *SIZES[:-1]), SIZES):
        pl.when((end > below) & (end <= size))(functools.partial(attend, size))


def cross_attention(kv, q, block=256):
    rows = kv.shape[0]
    nodes = q.shape[0]
    return pl.pallas_call(
        cross_kernel,
        grid=(nodes // block,),
        out_shape=jax.ShapeDtypeStruct(q.shape, BF16),
        in_specs=[
            pl.BlockSpec((rows, 2 * PAIR), lambda j: (0, 0)),
            pl.BlockSpec((block, PAIR), lambda j: (j, 0)),
        ],
        out_specs=pl.BlockSpec((block, PAIR), lambda j: (j, 0)),
        scratch_shapes=[
            pltpu.VMEM((rows + SPARE, 2 * PAIR), BF16),
            pltpu.VMEM((PAIR, rows), BF16),
            pltpu.VMEM((PAIR, rows), BF16),
            pltpu.VMEM((rows, PAIR), BF16),
            pltpu.VMEM((rows, PAIR), BF16),
            pltpu.VMEM((block, rows), F32),
            pltpu.VMEM((block, rows), F32),
            pltpu.SMEM((1,), jnp.int32),
        ],
        compiler_params=params(),
        name="cross_attention",
    )(kv, q)


def window_kernel(block, q, key, value, out, bias):
    nodes = q.shape[0]
    window = key.shape[0]
    half = (window - nodes) // 2
    wide = block + 2 * half
    me = (lax.axis_index("loc") * 4 + lax.axis_index("s0")) * 2 + lax.axis_index("s1")

    @pl.when(pl.program_id(0) == 0)
    def _():
        first = jnp.where(me == 0, half, 0)
        last = jnp.where(me == LOC * GROUPS - 1, half + nodes, window)
        row = lax.broadcasted_iota(jnp.int32, (block, wide), 0)
        column = lax.broadcasted_iota(jnp.int32, (block, wide), 1)
        near = (column >= row) & (column <= row + 2 * half)
        for b in range(nodes // block):
            there = (column + b * block >= first) & (column + b * block < last)
            bias[b] = jnp.where(near & there, 0.0, MASKED)

    values = value[...].astype(F32)
    low_values = lax.broadcasted_iota(jnp.int32, values.shape, 1) < HEAD
    v0 = jnp.where(low_values, values, 1.0).astype(BF16)
    v1 = jnp.where(low_values, 1.0, values).astype(BF16)
    low = lax.broadcasted_iota(jnp.int32, (block, PAIR), 1) < HEAD
    for b in range(nodes // block):
        both = q[b * block : (b + 1) * block, :].astype(F32)
        q0 = jnp.where(low, both, 0.0).astype(BF16)
        q1 = jnp.where(low, 0.0, both).astype(BF16)
        near = slice(b * block, b * block + wide)
        a0 = lax.dot_general(q0, key[near, :], NT, preferred_element_type=F32) + bias[b]
        a1 = lax.dot_general(q1, key[near, :], NT, preferred_element_type=F32) + bias[b]
        p0 = jnp.exp2(a0 - jnp.max(a0, axis=1, keepdims=True)).astype(BF16)
        p1 = jnp.exp2(a1 - jnp.max(a1, axis=1, keepdims=True)).astype(BF16)
        t0 = jnp.dot(p0, v0[near], preferred_element_type=F32)
        t1 = jnp.dot(p1, v1[near], preferred_element_type=F32)
        sums = pltpu.roll(jnp.where(low, t1, t0), HEAD, 1)
        out[b * block : (b + 1) * block, :] = (jnp.where(low, t0, t1) / sums).astype(BF16)


def window_attention(q, kv, block=192):
    nodes = q.shape[0]
    window = kv.shape[0]
    return pl.pallas_call(
        functools.partial(window_kernel, block),
        grid=(GROUPS,),
        out_shape=jax.ShapeDtypeStruct(q.shape, BF16),
        in_specs=[
            pl.BlockSpec((nodes, PAIR), lambda j: (0, j)),
            pl.BlockSpec((window, PAIR), lambda j: (0, j)),
            pl.BlockSpec((window, PAIR), lambda j: (0, j + GROUPS)),
        ],
        out_specs=pl.BlockSpec((nodes, PAIR), lambda j: (0, j)),
        scratch_shapes=[pltpu.VMEM((nodes // block, block, block + window - nodes), F32)],
        compiler_params=params(),
        name="window_attention",
    )(q, kv, kv)


def tail_kernel(
    ctx, before, self_out, weights, out,
    w_in, w_back, x, mine, other, total, part, got, w_sems, send, recv,
):
    loc = lax.axis_index("loc")
    z = lax.axis_index("s0")
    core = lax.axis_index("s1")
    chunks, devices = w_in.shape[0], w_in.shape[1]
    sibling = functools.partial(
        pltpu.make_async_remote_copy, device_id=(loc, z, 1 - core), device_id_type=MESH
    )

    def load(c):
        at = pl.ds(c * devices, devices)
        return (
            pltpu.make_async_copy(weights.at[at, 0], w_in.at[c], w_sems.at[0, c]),
            pltpu.make_async_copy(weights.at[at, 1], w_back.at[c], w_sems.at[1, c]),
        )

    for c in range(chunks):
        for copy in load(c):
            copy.start()
    barrier = pltpu.get_barrier_semaphore()
    pl.semaphore_signal(barrier, inc=1, device_id=(loc, z, 1 - core), device_id_type=MESH)

    mixed = jnp.dot(ctx[...], self_out[...], preferred_element_type=F32)
    after = (before[...].astype(F32) + mixed).astype(BF16)
    x[...] = after
    mine[...] = rms_norm(after)
    pl.semaphore_wait(barrier, 1)
    give = sibling(mine, other, send.at[0], recv.at[0])
    give.start()

    def mlp(rows, c):
        wide = devices * w_in.shape[2]
        first = w_in[c].reshape(wide, w_in.shape[3])
        second = w_back[c].reshape(wide, w_back.shape[3])
        hidden = lax.dot_general(rows[...], first, NT, preferred_element_type=F32)
        hidden = jax.nn.gelu(hidden, approximate=True).astype(BF16)
        return jnp.dot(hidden, second, preferred_element_type=F32)

    for copy in load(0):
        copy.wait()
    total[...] = mlp(mine, 0)
    give.wait_recv()
    part[...] = mlp(other, 0)
    for c in range(1, chunks):
        for copy in load(c):
            copy.wait()

    @pl.loop(1, chunks)
    def _(c):
        part[...] += mlp(other, c)

    back = sibling(part, got, send.at[1], recv.at[1])
    back.start()

    @pl.loop(1, chunks)
    def _(c):
        total[...] += mlp(mine, c)

    back.wait_recv()
    out[...] = (x[...].astype(F32) + (total[...] + got[...])).astype(BF16)
    give.wait_send()
    back.wait_send()


def tail(ctx, before, self_out, weights, chunks=4):
    nodes, width = ctx.shape
    devices, _, units, _ = weights.shape
    vmem = pl.BlockSpec(memory_space=pltpu.VMEM)
    block = (chunks, devices // chunks, units, width)
    return pl.pallas_call(
        tail_kernel,
        out_shape=jax.ShapeDtypeStruct(ctx.shape, BF16),
        in_specs=[vmem, vmem, vmem, pl.BlockSpec(memory_space=pl.ANY)],
        out_specs=vmem,
        scratch_shapes=[
            pltpu.VMEM(block, BF16),
            pltpu.VMEM(block, BF16),
            pltpu.VMEM((nodes, width), BF16),
            pltpu.VMEM((nodes, width), BF16),
            pltpu.VMEM((nodes, width), BF16),
            pltpu.VMEM((nodes, width), F32),
            pltpu.VMEM((nodes, width), F32),
            pltpu.VMEM((nodes, width), F32),
            pltpu.SemaphoreType.DMA((2, chunks)),
            pltpu.SemaphoreType.DMA((2,)),
            pltpu.SemaphoreType.DMA((2,)),
        ],
        compiler_params=params(has_side_effects=True, collective_id=3),
        name="tail",
    )(ctx, before, self_out, weights)


def shards(
    latent,
    observations,
    counts,
    cross_query,
    cross_kv,
    cross_out,
    self_qkv,
    self_out,
    mlp_in,
    mlp_out,
):
    nodes, width = latent.shape
    kv, q, column = project(
        counts.reshape(-1), observations.reshape(-1, width), latent, cross_kv, cross_query,
        mlp_in.T, mlp_out.T,
    )
    weights = lax.all_gather(column, "loc").reshape(-1, *column.shape[1:])
    kv_here, q_here = exchange(kv.reshape(LOC * GROUPS, CAP, 2 * PAIR), q)
    ctx = cross_attention(
        kv_here.reshape(-1, 2 * PAIR), q_here.reshape(-1, PAIR)
    )
    after_cross, self_q, self_kv = middle(
        latent, ctx.reshape(GROUPS, nodes, PAIR), cross_out, self_qkv
    )
    self_ctx = window_attention(self_q, self_kv)
    return tail(self_ctx, after_cross, self_out, weights)


def solution(mesh):
    finer = Mesh(mesh.devices.reshape(LOC, 4, 2), LOC_STREAM)
    return jax.shard_map(
        shards,
        mesh=finer,
        in_specs=(
            P(LOC_STREAM, None),
            P(STREAM, "loc", None, None, None),
            P(STREAM, "loc", None),
            P(),
            P(),
            P(),
            P(),
            P(),
            P(None, LOC_STREAM),
            P(None, LOC_STREAM),
        ),
        out_specs=P(LOC_STREAM, None),
        check_vma=False,
    )
```

```python
import functools
import math

import jax
import jax.numpy as jnp
from jax import lax
from jax.experimental import pallas as pl
from jax.experimental.pallas import tpu as pltpu
from jax.sharding import Mesh
from jax.sharding import PartitionSpec as P

HEADS = 16
HEAD = 64
PAIR = 128
GROUPS = 8
WIN = 512
LOC = 16
CAP = 32
STREAM = ("s0", "s1")
LOC_STREAM = ("loc", "s0", "s1")
EPSILON = 1e-06
MASKED = -1e30
PADDING = 1e30
PADDING_FROM = 1e29
QSCALE = math.log2(math.e) / math.sqrt(HEAD)
MESH = pl.DeviceIdType.MESH
F32 = jnp.float32
BF16 = jnp.bfloat16
NT = (((1,), (1,)), ((), ()))
VMEM_LIMIT = 56 << 20


def params(**more):
    return pltpu.CompilerParams(vmem_limit_bytes=VMEM_LIMIT, **more)


def rms_norm(tensor):
    floats = tensor.astype(F32)
    return (floats * lax.rsqrt(jnp.mean(floats * floats, axis=-1, keepdims=True) + EPSILON)).astype(
        BF16
    )


def project_kernel(
    counts, obs, latent, wk, wv, wq, w_in, w_back, kv_out, q_out, column,
    xn, ln, send, recv,
):
    loc = lax.axis_index("loc")
    z = lax.axis_index("s0")
    core = lax.axis_index("s1")
    step = pl.program_id(0)

    @pl.when(step == 0)
    def _():
        barrier = pltpu.get_barrier_semaphore()
        for d in range(1, 4):
            pl.semaphore_signal(
                barrier, inc=1, device_id=(loc, lax.rem(z + d, 4), core), device_id_type=MESH
            )
        xn[...] = rms_norm(obs[...])
        ln[...] = rms_norm(latent[...])

        pl.semaphore_wait(barrier, 3)
        for at, part in enumerate((w_in, w_back)):
            pltpu.make_async_copy(part, column.at[z, at], recv).start()
            for d in range(1, 4):
                pltpu.make_async_remote_copy(
                    part, column.at[z, at], send, recv,
                    device_id=(loc, lax.rem(z + d, 4), core), device_id_type=MESH,
                ).start()

    q = (jnp.dot(ln[...], wq[...], preferred_element_type=F32) * QSCALE).astype(BF16)
    k = jnp.dot(xn[...], wk[...], preferred_element_type=F32)
    v = jnp.dot(xn[...], wv[...], preferred_element_type=F32)
    slot = lax.broadcasted_iota(jnp.int32, (CAP, PAIR), 0)
    for s in range(LOC):
        live = slot < counts[s]
        rows = slice(s * CAP, (s + 1) * CAP)
        for g in range(2):
            columns = slice(g * PAIR, (g + 1) * PAIR)
            kv_out[s, g, :, 0:PAIR] = jnp.where(live, k[rows, columns], PADDING).astype(BF16)
            kv_out[s, g, :, PAIR:] = jnp.where(live, v[rows, columns], PADDING).astype(BF16)
    for g in range(2):
        q_out[g] = q[:, g * PAIR : (g + 1) * PAIR]

    @pl.when(step == pl.num_programs(0) - 1)
    def _():
        sent = column.at[pl.ds(0, 3)]
        pltpu.make_async_copy(sent, sent, send).wait()
        pltpu.make_async_copy(column, column, recv).wait()


def project(counts, obs, latent, cross_kv, cross_query, w_in, w_back):
    rows, width = obs.shape
    nodes = latent.shape[0]
    step = 2 * PAIR
    steps = width // step
    return pl.pallas_call(
        project_kernel,
        grid=(steps,),
        out_shape=(
            jax.ShapeDtypeStruct((LOC, GROUPS, CAP, 2 * PAIR), BF16),
            jax.ShapeDtypeStruct((GROUPS, nodes, PAIR), BF16),
            jax.ShapeDtypeStruct((4, 2, *w_in.shape), BF16),
        ),
        in_specs=[
            pl.BlockSpec(memory_space=pltpu.SMEM),
            pl.BlockSpec((rows, width), lambda j: (0, 0)),
            pl.BlockSpec((nodes, width), lambda j: (0, 0)),
            pl.BlockSpec((width, step), lambda j: (0, j)),
            pl.BlockSpec((width, step), lambda j: (0, j + steps)),
            pl.BlockSpec((width, step), lambda j: (0, j)),
            pl.BlockSpec(memory_space=pl.ANY),
            pl.BlockSpec(memory_space=pl.ANY),
        ],
        out_specs=(
            pl.BlockSpec((LOC, 2, CAP, 2 * PAIR), lambda j: (0, j, 0, 0)),
            pl.BlockSpec((2, nodes, PAIR), lambda j: (j, 0, 0)),
            pl.BlockSpec(memory_space=pl.ANY),
        ),
        scratch_shapes=[
            pltpu.VMEM((rows, width), BF16),
            pltpu.VMEM((nodes, width), BF16),
            pltpu.SemaphoreType.DMA,
            pltpu.SemaphoreType.DMA,
        ],
        compiler_params=params(has_side_effects=True, collective_id=2),
        name="project",
    )(counts, obs, latent, cross_kv, cross_kv, cross_query, w_in, w_back)


def exchange_kernel(kv, q, kv_here, q_here, kv_send, kv_recv, q_send, q_recv):
    loc = lax.axis_index("loc")
    me = lax.axis_index("s0") * 2 + lax.axis_index("s1")
    mine = loc * GROUPS + me
    pltpu.make_async_copy(q.at[me], q_here.at[me], q_recv).start()
    pltpu.make_async_copy(kv.at[mine], kv_here.at[me * LOC + loc], kv_recv).start()

    @pl.loop(1, GROUPS)
    def _(d):
        to = lax.rem(me + d, GROUPS)
        pltpu.make_async_remote_copy(
            q.at[to],
            q_here.at[me],
            q_send,
            q_recv,
            device_id=(loc, to // 2, lax.rem(to, 2)),
            device_id_type=MESH,
        ).start()

    @pl.loop(1, LOC * GROUPS)
    def _(d):
        to = lax.rem(mine + d * 37, LOC * GROUPS)
        section = to // GROUPS
        group = lax.rem(to, GROUPS)
        pltpu.make_async_remote_copy(
            kv.at[to],
            kv_here.at[me * LOC + loc],
            kv_send,
            kv_recv,
            device_id=(section, group // 2, lax.rem(group, 2)),
            device_id_type=MESH,
        ).start()

    pltpu.make_async_copy(q.at[pl.ds(0, GROUPS - 1)], q_here.at[pl.ds(0, GROUPS - 1)], q_send).wait()
    pltpu.make_async_copy(q, q_here, q_recv).wait()

    sent = pl.ds(0, LOC * GROUPS - 1)
    pltpu.make_async_copy(kv.at[sent], kv_here.at[sent], kv_send).wait()
    pltpu.make_async_copy(kv_here, kv_here, kv_recv).wait()


def exchange(kv, q):
    return pl.pallas_call(
        exchange_kernel,
        out_shape=(
            jax.ShapeDtypeStruct(kv.shape, BF16),
            jax.ShapeDtypeStruct(q.shape, BF16),
        ),
        in_specs=[pl.BlockSpec(memory_space=pl.ANY)] * 2,
        out_specs=(pl.BlockSpec(memory_space=pl.ANY),) * 2,
        scratch_shapes=[pltpu.SemaphoreType.DMA] * 4,
        compiler_params=params(has_side_effects=True),
        name="exchange",
    )(kv, q)


def middle_kernel(
    latent, ctx, cross_out, self_qkv, after, q, kv,
    mixed, w_out, w_qkv, low, high, normed, w_sems, ctx_send, ctx_recv, send, recv,
):
    loc = lax.axis_index("loc")
    me = lax.axis_index("s0") * 2 + lax.axis_index("s1")
    flat = loc * GROUPS + me
    nodes, width = latent.shape
    half = low.shape[0]
    starts, ends = flat == 0, flat == LOC * GROUPS - 1
    outer_low = (me == 0) & jnp.logical_not(starts)
    outer_high = (me == GROUPS - 1) & jnp.logical_not(ends)

    def device(index):
        group = lax.rem(index, GROUPS)
        return index // GROUPS, group // 2, lax.rem(group, 2)

    load_out = pltpu.make_async_copy(cross_out, w_out, w_sems.at[0])
    load_qkv = pltpu.make_async_copy(self_qkv, w_qkv, w_sems.at[1])
    load_out.start()
    load_qkv.start()

    barrier = pltpu.get_barrier_semaphore()

    @pl.loop(1, GROUPS)
    def _(d):
        to = lax.rem(me + d, GROUPS)
        pl.semaphore_signal(
            barrier, inc=1, device_id=(loc, to // 2, lax.rem(to, 2)), device_id_type=MESH
        )

    @pl.when(outer_low)
    def _():
        pl.semaphore_signal(barrier, inc=1, device_id=device(flat - 1), device_id_type=MESH)

    @pl.when(outer_high)
    def _():
        pl.semaphore_signal(barrier, inc=1, device_id=device(flat + 1), device_id_type=MESH)

    pl.semaphore_wait(
        barrier, GROUPS - 1 + outer_low.astype(jnp.int32) + outer_high.astype(jnp.int32)
    )

    place = mixed.at[:, pl.ds(pl.multiple_of(me * PAIR, PAIR), PAIR)]

    @pl.loop(1, GROUPS)
    def _(d):
        to = lax.rem(me + d, GROUPS)
        pltpu.make_async_remote_copy(
            ctx.at[to],
            place,
            ctx_send,
            ctx_recv,
            device_id=(loc, to // 2, lax.rem(to, 2)),
            device_id_type=MESH,
        ).start()

    pltpu.make_async_copy(ctx.at[me], place, ctx_recv).start()

    @pl.when(starts)
    def _():
        low[...] = jnp.zeros_like(low)

    @pl.when(ends)
    def _():
        high[...] = jnp.zeros_like(high)

    load_out.wait()
    pltpu.make_async_copy(mixed, mixed, ctx_recv).wait()
    after[...] = (
        latent[...].astype(F32) + jnp.dot(mixed[...], w_out[...], preferred_element_type=F32)
    ).astype(BF16)

    down = pltpu.make_async_remote_copy(
        after.at[0:half], high, send.at[0], recv.at[1],
        device_id=device(jnp.maximum(flat - 1, 0)), device_id_type=MESH,
    )
    up = pltpu.make_async_remote_copy(
        after.at[nodes - half : nodes], low, send.at[1], recv.at[0],
        device_id=device(jnp.minimum(flat + 1, LOC * GROUPS - 1)), device_id_type=MESH,
    )
    pl.when(jnp.logical_not(starts))(down.start)
    pl.when(jnp.logical_not(ends))(up.start)

    normed[...] = rms_norm(after[...])
    load_qkv.wait()
    step = 512

    @pl.loop(0, width // step)
    def _(c):
        at = pl.ds(pl.multiple_of(c * step, step), step)
        found = jnp.dot(normed[...], w_qkv[:, at], preferred_element_type=F32)
        q[:, at] = (found * QSCALE).astype(BF16)

    def project(rows, to):
        @pl.loop(0, 2 * width // step)
        def _(c):
            at = pl.ds(pl.multiple_of(c * step, step), step)
            weights = w_qkv[:, pl.ds(pl.multiple_of(width + c * step, step), step)]
            kv[to, at] = jnp.dot(rows[...], weights, preferred_element_type=F32).astype(BF16)

    project(normed, slice(half, half + nodes))

    @pl.when(jnp.logical_not(starts))
    def _():
        pltpu.make_async_copy(low, low, recv.at[0]).wait()

    normed[0:half] = rms_norm(low[...])
    project(normed.at[0:half], slice(0, half))

    @pl.when(jnp.logical_not(ends))
    def _():
        pltpu.make_async_copy(high, high, recv.at[1]).wait()

    normed[0:half] = rms_norm(high[...])
    project(normed.at[0:half], slice(half + nodes, 2 * half + nodes))

    pl.when(jnp.logical_not(starts))(down.wait_send)
    pl.when(jnp.logical_not(ends))(up.wait_send)
    sent = ctx.at[pl.ds(0, GROUPS - 1)]
    pltpu.make_async_copy(sent, sent, ctx_send).wait()


def middle(latent, ctx, cross_out, self_qkv):
    nodes, width = latent.shape
    half = WIN // 2
    vmem = pl.BlockSpec(memory_space=pltpu.VMEM)
    away = pl.BlockSpec(memory_space=pl.ANY)
    return pl.pallas_call(
        middle_kernel,
        out_shape=(
            jax.ShapeDtypeStruct((nodes, width), BF16),
            jax.ShapeDtypeStruct((nodes, width), BF16),
            jax.ShapeDtypeStruct((nodes + WIN, 2 * width), BF16),
        ),
        in_specs=[vmem, away, away, away],
        out_specs=(vmem, vmem, vmem),
        scratch_shapes=[
            pltpu.VMEM((nodes, width), BF16),
            pltpu.VMEM((width, width), BF16),
            pltpu.VMEM((width, 3 * width), BF16),
            pltpu.VMEM((half, width), BF16),
            pltpu.VMEM((half, width), BF16),
            pltpu.VMEM((nodes, width), BF16),
            pltpu.SemaphoreType.DMA((2,)),
            pltpu.SemaphoreType.DMA,
            pltpu.SemaphoreType.DMA,
            pltpu.SemaphoreType.DMA((2,)),
            pltpu.SemaphoreType.DMA((2,)),
        ],
        compiler_params=params(has_side_effects=True, collective_id=1),
        name="middle",
    )(latent, ctx, cross_out, self_qkv)


PACK = 512
SIZES = (1536, 1792, 2048, 2304, 2560, 2816, 3072, 3584, 4096)
SPARE = 1536


def lane_max(scores, width):
    top = scores[:, 0:PAIR]
    for c in range(1, width // PAIR):
        top = jnp.maximum(top, scores[:, c * PAIR : (c + 1) * PAIR])
    return top


def pack_rows(kv, packed):
    groups = kv.shape[0] // PACK
    row = lax.broadcasted_iota(jnp.int32, (PACK, PACK), 0)
    column = lax.broadcasted_iota(jnp.int32, (PACK, PACK), 1)
    slot = lax.broadcasted_iota(jnp.int32, (PACK, 2 * PAIR), 0)
    earlier = (row < column).astype(BF16)
    lives = []
    for g in range(groups):
        key = kv[g * PACK : (g + 1) * PACK, 0:PAIR].astype(F32)
        lives.append(jnp.transpose(jnp.where(key < PADDING_FROM, 1.0, 0.0))[0:1, :])
    live = jnp.concatenate(lives, axis=0)
    before = jnp.dot(live.astype(BF16), earlier, preferred_element_type=F32)
    places = jnp.where(live > 0.5, before, -1.0).astype(jnp.int32)
    end = 0
    for g in range(groups):
        number = jnp.sum(live[g : g + 1, :]).astype(jnp.int32)
        pick = (places[g : g + 1, :] == row).astype(BF16)
        found = jnp.dot(pick, kv[g * PACK : (g + 1) * PACK, :], preferred_element_type=F32)
        packed[pl.ds(pl.multiple_of(end, 16), PACK), :] = jnp.where(
            slot < number, found, PADDING
        ).astype(BF16)
        end = end + (number + 15) // 16 * 16
    packed[pl.ds(pl.multiple_of(end, 16), SPARE), :] = jnp.full((SPARE, 2 * PAIR), PADDING, BF16)
    return end


def cross_kernel(kv, q, out, packed, k0, k1, v0, v1, s0, s1, length):
    block = q.shape[0]

    @pl.when(pl.program_id(0) == 0)
    def _():
        end = pack_rows(kv, packed)
        length[0] = end
        lane = lax.broadcasted_iota(jnp.int32, (PACK, PAIR), 1)
        low = lane < HEAD

        @pl.loop(0, jnp.maximum((end + PACK - 1) // PACK, SIZES[0] // PACK))
        def _(b):
            at = pl.ds(pl.multiple_of(b * PACK, PACK), PACK)
            key = packed[at, 0:PAIR].astype(F32)
            value = packed[at, PAIR:].astype(F32)
            live = key < PADDING_FROM
            bias = jnp.where(live, 0.0, MASKED)
            key = jnp.where(live, key, 0.0)
            value = jnp.where(live, value, 0.0)
            first = jnp.where(low, key, jnp.where(lane == HEAD, bias, 0.0))
            second = jnp.where(low, jnp.where(lane == 0, bias, 0.0), key)
            k0[:, at] = jnp.transpose(first).astype(BF16)
            k1[:, at] = jnp.transpose(second).astype(BF16)
            v0[at, :] = jnp.where(low, value, 1.0).astype(BF16)
            v1[at, :] = jnp.where(low, 1.0, value).astype(BF16)

    end = length[0]

    def attend(size):
        lane = lax.broadcasted_iota(jnp.int32, (block, PAIR), 1)
        low = lane < HEAD
        both = q[...].astype(F32)
        q0 = jnp.where(low, both, jnp.where(lane == HEAD, 1.0, 0.0)).astype(BF16)
        q1 = jnp.where(low, jnp.where(lane == 0, 1.0, 0.0), both).astype(BF16)
        step = 512
        chunks = [slice(at, min(at + step, size)) for at in range(0, size, step)]
        lowest = jnp.full((block, PAIR), -3e38, F32)
        zero = jnp.zeros((block, PAIR), F32)

        def score(query, k, s, at, top):
            scores = jnp.dot(query, k[:, at], preferred_element_type=F32)
            s[:, at] = scores
            return jnp.maximum(top, lane_max(scores, at.stop - at.start))

        def mix(s, v, top, at, total):
            weights = jnp.exp2(s[:, at] - top).astype(BF16)
            return total + jnp.dot(weights, v[at, :], preferred_element_type=F32)

        top0, top1, t0, t1 = lowest, lowest, zero, zero
        for at in chunks:
            top0 = score(q0, k0, s0, at, top0)
        top0 = jnp.max(top0, axis=1, keepdims=True)
        for at in chunks:
            top1 = score(q1, k1, s1, at, top1)
            t0 = mix(s0, v0, top0, at, t0)
        top1 = jnp.max(top1, axis=1, keepdims=True)
        for at in chunks:
            t1 = mix(s1, v1, top1, at, t1)
        sums = pltpu.roll(jnp.where(low, t1, t0), HEAD, 1)
        out[...] = (jnp.where(low, t0, t1) / sums).astype(BF16)

    for below, size in zip((0, *SIZES[:-1]), SIZES):
        pl.when((end > below) & (end <= size))(functools.partial(attend, size))


def cross_attention(kv, q, block=512):
    rows = kv.shape[0]
    nodes = q.shape[0]
    return pl.pallas_call(
        cross_kernel,
        grid=(nodes // block,),
        out_shape=jax.ShapeDtypeStruct(q.shape, BF16),
        in_specs=[
            pl.BlockSpec((rows, 2 * PAIR), lambda j: (0, 0)),
            pl.BlockSpec((block, PAIR), lambda j: (j, 0)),
        ],
        out_specs=pl.BlockSpec((block, PAIR), lambda j: (j, 0)),
        scratch_shapes=[
            pltpu.VMEM((rows + SPARE, 2 * PAIR), BF16),
            pltpu.VMEM((PAIR, rows), BF16),
            pltpu.VMEM((PAIR, rows), BF16),
            pltpu.VMEM((rows, PAIR), BF16),
            pltpu.VMEM((rows, PAIR), BF16),
            pltpu.VMEM((block, rows), F32),
            pltpu.VMEM((block, rows), F32),
            pltpu.SMEM((1,), jnp.int32),
        ],
        compiler_params=params(),
        name="cross_attention",
    )(kv, q)


def window_kernel(block, q, key, value, out, bias):
    nodes = q.shape[0]
    window = key.shape[0]
    half = (window - nodes) // 2
    wide = block + 2 * half
    me = (lax.axis_index("loc") * 4 + lax.axis_index("s0")) * 2 + lax.axis_index("s1")

    @pl.when(pl.program_id(0) == 0)
    def _():
        first = jnp.where(me == 0, half, 0)
        last = jnp.where(me == LOC * GROUPS - 1, half + nodes, window)
        row = lax.broadcasted_iota(jnp.int32, (block, wide), 0)
        column = lax.broadcasted_iota(jnp.int32, (block, wide), 1)
        near = (column >= row) & (column <= row + 2 * half)
        for b in range(nodes // block):
            there = (column + b * block >= first) & (column + b * block < last)
            bias[b] = jnp.where(near & there, 0.0, MASKED)

    values = value[...].astype(F32)
    low_values = lax.broadcasted_iota(jnp.int32, values.shape, 1) < HEAD
    v0 = jnp.where(low_values, values, 1.0).astype(BF16)
    v1 = jnp.where(low_values, 1.0, values).astype(BF16)
    low = lax.broadcasted_iota(jnp.int32, (block, PAIR), 1) < HEAD
    for b in range(nodes // block):
        both = q[b * block : (b + 1) * block, :].astype(F32)
        q0 = jnp.where(low, both, 0.0).astype(BF16)
        q1 = jnp.where(low, 0.0, both).astype(BF16)
        near = slice(b * block, b * block + wide)
        a0 = lax.dot_general(q0, key[near, :], NT, preferred_element_type=F32) + bias[b]
        a1 = lax.dot_general(q1, key[near, :], NT, preferred_element_type=F32) + bias[b]
        p0 = jnp.exp2(a0 - jnp.max(a0, axis=1, keepdims=True)).astype(BF16)
        p1 = jnp.exp2(a1 - jnp.max(a1, axis=1, keepdims=True)).astype(BF16)
        t0 = jnp.dot(p0, v0[near], preferred_element_type=F32)
        t1 = jnp.dot(p1, v1[near], preferred_element_type=F32)
        sums = pltpu.roll(jnp.where(low, t1, t0), HEAD, 1)
        out[b * block : (b + 1) * block, :] = (jnp.where(low, t0, t1) / sums).astype(BF16)


def window_attention(q, kv, block=192):
    nodes = q.shape[0]
    window = kv.shape[0]
    return pl.pallas_call(
        functools.partial(window_kernel, block),
        grid=(GROUPS,),
        out_shape=jax.ShapeDtypeStruct(q.shape, BF16),
        in_specs=[
            pl.BlockSpec((nodes, PAIR), lambda j: (0, j)),
            pl.BlockSpec((window, PAIR), lambda j: (0, j)),
            pl.BlockSpec((window, PAIR), lambda j: (0, j + GROUPS)),
        ],
        out_specs=pl.BlockSpec((nodes, PAIR), lambda j: (0, j)),
        scratch_shapes=[pltpu.VMEM((nodes // block, block, block + window - nodes), F32)],
        compiler_params=params(),
        name="window_attention",
    )(q, kv, kv)


def tail_kernel(
    ctx, before, self_out, weights, out,
    w_in, w_back, x, mine, other, total, part, got, w_sems, send, recv,
):
    loc = lax.axis_index("loc")
    z = lax.axis_index("s0")
    core = lax.axis_index("s1")
    chunks, devices = w_in.shape[0], w_in.shape[1]
    sibling = functools.partial(
        pltpu.make_async_remote_copy, device_id=(loc, z, 1 - core), device_id_type=MESH
    )

    def load(c):
        at = pl.ds(c * devices, devices)
        return (
            pltpu.make_async_copy(weights.at[at, 0], w_in.at[c], w_sems.at[0, c]),
            pltpu.make_async_copy(weights.at[at, 1], w_back.at[c], w_sems.at[1, c]),
        )

    for c in range(chunks):
        for copy in load(c):
            copy.start()
    barrier = pltpu.get_barrier_semaphore()
    pl.semaphore_signal(barrier, inc=1, device_id=(loc, z, 1 - core), device_id_type=MESH)

    mixed = jnp.dot(ctx[...], self_out[...], preferred_element_type=F32)
    after = (before[...].astype(F32) + mixed).astype(BF16)
    x[...] = after
    mine[...] = rms_norm(after)
    pl.semaphore_wait(barrier, 1)
    give = sibling(mine, other, send.at[0], recv.at[0])
    give.start()

    def mlp(rows, c):
        wide = devices * w_in.shape[2]
        first = w_in[c].reshape(wide, w_in.shape[3])
        second = w_back[c].reshape(wide, w_back.shape[3])
        hidden = lax.dot_general(rows[...], first, NT, preferred_element_type=F32)
        hidden = jax.nn.gelu(hidden, approximate=True).astype(BF16)
        return jnp.dot(hidden, second, preferred_element_type=F32)

    for copy in load(0):
        copy.wait()
    total[...] = mlp(mine, 0)
    give.wait_recv()
    part[...] = mlp(other, 0)
    for c in range(1, chunks):
        for copy in load(c):
            copy.wait()

    @pl.loop(1, chunks)
    def _(c):
        part[...] += mlp(other, c)

    back = sibling(part, got, send.at[1], recv.at[1])
    back.start()

    @pl.loop(1, chunks)
    def _(c):
        total[...] += mlp(mine, c)

    back.wait_recv()
    out[...] = (x[...].astype(F32) + (total[...] + got[...])).astype(BF16)
    give.wait_send()
    back.wait_send()


def tail(ctx, before, self_out, weights, chunks=4):
    nodes, width = ctx.shape
    devices, _, units, _ = weights.shape
    vmem = pl.BlockSpec(memory_space=pltpu.VMEM)
    block = (chunks, devices // chunks, units, width)
    return pl.pallas_call(
        tail_kernel,
        out_shape=jax.ShapeDtypeStruct(ctx.shape, BF16),
        in_specs=[vmem, vmem, vmem, pl.BlockSpec(memory_space=pl.ANY)],
        out_specs=vmem,
        scratch_shapes=[
            pltpu.VMEM(block, BF16),
            pltpu.VMEM(block, BF16),
            pltpu.VMEM((nodes, width), BF16),
            pltpu.VMEM((nodes, width), BF16),
            pltpu.VMEM((nodes, width), BF16),
            pltpu.VMEM((nodes, width), F32),
            pltpu.VMEM((nodes, width), F32),
            pltpu.VMEM((nodes, width), F32),
            pltpu.SemaphoreType.DMA((2, chunks)),
            pltpu.SemaphoreType.DMA((2,)),
            pltpu.SemaphoreType.DMA((2,)),
        ],
        compiler_params=params(has_side_effects=True, collective_id=3),
        name="tail",
    )(ctx, before, self_out, weights)


def shards(
    latent,
    observations,
    counts,
    cross_query,
    cross_kv,
    cross_out,
    self_qkv,
    self_out,
    mlp_in,
    mlp_out,
):
    nodes, width = latent.shape
    kv, q, column = project(
        counts.reshape(-1), observations.reshape(-1, width), latent, cross_kv, cross_query,
        mlp_in.T, mlp_out.T,
    )
    weights = lax.all_gather(column, "loc").reshape(-1, *column.shape[1:])
    kv_here, q_here = exchange(kv.reshape(LOC * GROUPS, CAP, 2 * PAIR), q)
    ctx = cross_attention(
        kv_here.reshape(-1, 2 * PAIR), q_here.reshape(-1, PAIR)
    )
    after_cross, self_q, self_kv = middle(
        latent, ctx.reshape(GROUPS, nodes, PAIR), cross_out, self_qkv
    )
    self_ctx = window_attention(self_q, self_kv)
    return tail(self_ctx, after_cross, self_out, weights)


def solution(mesh):
    finer = Mesh(mesh.devices.reshape(LOC, 4, 2), LOC_STREAM)
    return jax.shard_map(
        shards,
        mesh=finer,
        in_specs=(
            P(LOC_STREAM, None),
            P(STREAM, "loc", None, None, None),
            P(STREAM, "loc", None),
            P(),
            P(),
            P(),
            P(),
            P(),
            P(None, LOC_STREAM),
            P(None, LOC_STREAM),
        ),
        out_specs=P(LOC_STREAM, None),
        check_vma=False,
    )
```

```python
import functools
import math

import jax
import jax.numpy as jnp
from jax import lax
from jax.experimental import pallas as pl
from jax.experimental.pallas import tpu as pltpu
from jax.sharding import Mesh
from jax.sharding import PartitionSpec as P

HEADS = 16
HEAD = 64
PAIR = 128
GROUPS = 8
WIN = 512
LOC = 16
CAP = 32
STREAM = ("s0", "s1")
LOC_STREAM = ("loc", "s0", "s1")
EPSILON = 1e-06
MASKED = -1e30
PADDING = 1e30
PADDING_FROM = 1e29
QSCALE = math.log2(math.e) / math.sqrt(HEAD)
MESH = pl.DeviceIdType.MESH
F32 = jnp.float32
BF16 = jnp.bfloat16
NT = (((1,), (1,)), ((), ()))
VMEM_LIMIT = 56 << 20


def params(**more):
    return pltpu.CompilerParams(vmem_limit_bytes=VMEM_LIMIT, **more)


def rms_norm(tensor):
    floats = tensor.astype(F32)
    return (floats * lax.rsqrt(jnp.mean(floats * floats, axis=-1, keepdims=True) + EPSILON)).astype(
        BF16
    )


def project_kernel(
    counts, obs, latent, wk, wv, wq, w_in, w_back, kv_out, q_out, column,
    xn, ln, send, recv,
):
    loc = lax.axis_index("loc")
    z = lax.axis_index("s0")
    core = lax.axis_index("s1")
    step = pl.program_id(0)

    @pl.when(step == 0)
    def _():
        barrier = pltpu.get_barrier_semaphore()
        for d in range(1, 4):
            pl.semaphore_signal(
                barrier, inc=1, device_id=(loc, lax.rem(z + d, 4), core), device_id_type=MESH
            )
        xn[...] = rms_norm(obs[...])
        ln[...] = rms_norm(latent[...])

        pl.semaphore_wait(barrier, 3)
        for at, part in enumerate((w_in, w_back)):
            pltpu.make_async_copy(part, column.at[z, at], recv).start()
            for d in range(1, 4):
                pltpu.make_async_remote_copy(
                    part, column.at[z, at], send, recv,
                    device_id=(loc, lax.rem(z + d, 4), core), device_id_type=MESH,
                ).start()

    q = (jnp.dot(ln[...], wq[...], preferred_element_type=F32) * QSCALE).astype(BF16)
    k = jnp.dot(xn[...], wk[...], preferred_element_type=F32)
    v = jnp.dot(xn[...], wv[...], preferred_element_type=F32)
    slot = lax.broadcasted_iota(jnp.int32, (CAP, PAIR), 0)
    for s in range(LOC):
        live = slot < counts[s]
        rows = slice(s * CAP, (s + 1) * CAP)
        for g in range(2):
            columns = slice(g * PAIR, (g + 1) * PAIR)
            kv_out[s, g, :, 0:PAIR] = jnp.where(live, k[rows, columns], PADDING).astype(BF16)
            kv_out[s, g, :, PAIR:] = jnp.where(live, v[rows, columns], PADDING).astype(BF16)
    for g in range(2):
        q_out[g] = q[:, g * PAIR : (g + 1) * PAIR]

    @pl.when(step == pl.num_programs(0) - 1)
    def _():
        sent = column.at[pl.ds(0, 3)]
        pltpu.make_async_copy(sent, sent, send).wait()
        pltpu.make_async_copy(column, column, recv).wait()


def project(counts, obs, latent, cross_kv, cross_query, w_in, w_back):
    rows, width = obs.shape
    nodes = latent.shape[0]
    step = 2 * PAIR
    steps = width // step
    return pl.pallas_call(
        project_kernel,
        grid=(steps,),
        out_shape=(
            jax.ShapeDtypeStruct((LOC, GROUPS, CAP, 2 * PAIR), BF16),
            jax.ShapeDtypeStruct((GROUPS, nodes, PAIR), BF16),
            jax.ShapeDtypeStruct((4, 2, *w_in.shape), BF16),
        ),
        in_specs=[
            pl.BlockSpec(memory_space=pltpu.SMEM),
            pl.BlockSpec((rows, width), lambda j: (0, 0)),
            pl.BlockSpec((nodes, width), lambda j: (0, 0)),
            pl.BlockSpec((width, step), lambda j: (0, j)),
            pl.BlockSpec((width, step), lambda j: (0, j + steps)),
            pl.BlockSpec((width, step), lambda j: (0, j)),
            pl.BlockSpec(memory_space=pl.ANY),
            pl.BlockSpec(memory_space=pl.ANY),
        ],
        out_specs=(
            pl.BlockSpec((LOC, 2, CAP, 2 * PAIR), lambda j: (0, j, 0, 0)),
            pl.BlockSpec((2, nodes, PAIR), lambda j: (j, 0, 0)),
            pl.BlockSpec(memory_space=pl.ANY),
        ),
        scratch_shapes=[
            pltpu.VMEM((rows, width), BF16),
            pltpu.VMEM((nodes, width), BF16),
            pltpu.SemaphoreType.DMA,
            pltpu.SemaphoreType.DMA,
        ],
        compiler_params=params(has_side_effects=True, collective_id=2),
        name="project",
    )(counts, obs, latent, cross_kv, cross_kv, cross_query, w_in, w_back)


def exchange_kernel(kv, q, kv_here, q_here, kv_send, kv_recv, q_send, q_recv):
    loc = lax.axis_index("loc")
    me = lax.axis_index("s0") * 2 + lax.axis_index("s1")
    mine = loc * GROUPS + me
    pltpu.make_async_copy(q.at[me], q_here.at[me], q_recv).start()
    pltpu.make_async_copy(kv.at[mine], kv_here.at[me * LOC + loc], kv_recv).start()

    @pl.loop(1, GROUPS)
    def _(d):
        to = lax.rem(me + d, GROUPS)
        pltpu.make_async_remote_copy(
            q.at[to],
            q_here.at[me],
            q_send,
            q_recv,
            device_id=(loc, to // 2, lax.rem(to, 2)),
            device_id_type=MESH,
        ).start()

    @pl.loop(1, LOC * GROUPS)
    def _(d):
        to = lax.rem(mine + d * 37, LOC * GROUPS)
        section = to // GROUPS
        group = lax.rem(to, GROUPS)
        pltpu.make_async_remote_copy(
            kv.at[to],
            kv_here.at[me * LOC + loc],
            kv_send,
            kv_recv,
            device_id=(section, group // 2, lax.rem(group, 2)),
            device_id_type=MESH,
        ).start()

    pltpu.make_async_copy(q.at[pl.ds(0, GROUPS - 1)], q_here.at[pl.ds(0, GROUPS - 1)], q_send).wait()
    pltpu.make_async_copy(q, q_here, q_recv).wait()

    sent = pl.ds(0, LOC * GROUPS - 1)
    pltpu.make_async_copy(kv.at[sent], kv_here.at[sent], kv_send).wait()
    pltpu.make_async_copy(kv_here, kv_here, kv_recv).wait()


def exchange(kv, q):
    return pl.pallas_call(
        exchange_kernel,
        out_shape=(
            jax.ShapeDtypeStruct(kv.shape, BF16),
            jax.ShapeDtypeStruct(q.shape, BF16),
        ),
        in_specs=[pl.BlockSpec(memory_space=pl.ANY)] * 2,
        out_specs=(pl.BlockSpec(memory_space=pl.ANY),) * 2,
        scratch_shapes=[pltpu.SemaphoreType.DMA] * 4,
        compiler_params=params(has_side_effects=True),
        name="exchange",
    )(kv, q)


def middle_kernel(
    latent, ctx, cross_out, self_qkv, after, q, kv,
    mixed, w_out, w_qkv, low, high, normed, w_sems, ctx_send, ctx_recv, send, recv,
):
    loc = lax.axis_index("loc")
    me = lax.axis_index("s0") * 2 + lax.axis_index("s1")
    flat = loc * GROUPS + me
    nodes, width = latent.shape
    half = low.shape[0]
    starts, ends = flat == 0, flat == LOC * GROUPS - 1
    outer_low = (me == 0) & jnp.logical_not(starts)
    outer_high = (me == GROUPS - 1) & jnp.logical_not(ends)

    def device(index):
        group = lax.rem(index, GROUPS)
        return index // GROUPS, group // 2, lax.rem(group, 2)

    load_out = pltpu.make_async_copy(cross_out, w_out, w_sems.at[0])
    load_qkv = pltpu.make_async_copy(self_qkv, w_qkv, w_sems.at[1])
    load_out.start()
    load_qkv.start()

    barrier = pltpu.get_barrier_semaphore()

    @pl.loop(1, GROUPS)
    def _(d):
        to = lax.rem(me + d, GROUPS)
        pl.semaphore_signal(
            barrier, inc=1, device_id=(loc, to // 2, lax.rem(to, 2)), device_id_type=MESH
        )

    @pl.when(outer_low)
    def _():
        pl.semaphore_signal(barrier, inc=1, device_id=device(flat - 1), device_id_type=MESH)

    @pl.when(outer_high)
    def _():
        pl.semaphore_signal(barrier, inc=1, device_id=device(flat + 1), device_id_type=MESH)

    pl.semaphore_wait(
        barrier, GROUPS - 1 + outer_low.astype(jnp.int32) + outer_high.astype(jnp.int32)
    )

    place = mixed.at[:, pl.ds(pl.multiple_of(me * PAIR, PAIR), PAIR)]

    @pl.loop(1, GROUPS)
    def _(d):
        to = lax.rem(me + d, GROUPS)
        pltpu.make_async_remote_copy(
            ctx.at[to],
            place,
            ctx_send,
            ctx_recv,
            device_id=(loc, to // 2, lax.rem(to, 2)),
            device_id_type=MESH,
        ).start()

    pltpu.make_async_copy(ctx.at[me], place, ctx_recv).start()

    @pl.when(starts)
    def _():
        low[...] = jnp.zeros_like(low)

    @pl.when(ends)
    def _():
        high[...] = jnp.zeros_like(high)

    load_out.wait()
    pltpu.make_async_copy(mixed, mixed, ctx_recv).wait()
    after[...] = (
        latent[...].astype(F32) + jnp.dot(mixed[...], w_out[...], preferred_element_type=F32)
    ).astype(BF16)

    down = pltpu.make_async_remote_copy(
        after.at[0:half], high, send.at[0], recv.at[1],
        device_id=device(jnp.maximum(flat - 1, 0)), device_id_type=MESH,
    )
    up = pltpu.make_async_remote_copy(
        after.at[nodes - half : nodes], low, send.at[1], recv.at[0],
        device_id=device(jnp.minimum(flat + 1, LOC * GROUPS - 1)), device_id_type=MESH,
    )
    pl.when(jnp.logical_not(starts))(down.start)
    pl.when(jnp.logical_not(ends))(up.start)

    normed[...] = rms_norm(after[...])
    load_qkv.wait()
    step = 512

    @pl.loop(0, width // step)
    def _(c):
        at = pl.ds(pl.multiple_of(c * step, step), step)
        found = jnp.dot(normed[...], w_qkv[:, at], preferred_element_type=F32)
        q[:, at] = (found * QSCALE).astype(BF16)

    def project(rows, to):
        @pl.loop(0, 2 * width // step)
        def _(c):
            at = pl.ds(pl.multiple_of(c * step, step), step)
            weights = w_qkv[:, pl.ds(pl.multiple_of(width + c * step, step), step)]
            kv[to, at] = jnp.dot(rows[...], weights, preferred_element_type=F32).astype(BF16)

    project(normed, slice(half, half + nodes))

    @pl.when(jnp.logical_not(starts))
    def _():
        pltpu.make_async_copy(low, low, recv.at[0]).wait()

    normed[0:half] = rms_norm(low[...])
    project(normed.at[0:half], slice(0, half))

    @pl.when(jnp.logical_not(ends))
    def _():
        pltpu.make_async_copy(high, high, recv.at[1]).wait()

    normed[0:half] = rms_norm(high[...])
    project(normed.at[0:half], slice(half + nodes, 2 * half + nodes))

    pl.when(jnp.logical_not(starts))(down.wait_send)
    pl.when(jnp.logical_not(ends))(up.wait_send)
    sent = ctx.at[pl.ds(0, GROUPS - 1)]
    pltpu.make_async_copy(sent, sent, ctx_send).wait()


def middle(latent, ctx, cross_out, self_qkv):
    nodes, width = latent.shape
    half = WIN // 2
    vmem = pl.BlockSpec(memory_space=pltpu.VMEM)
    away = pl.BlockSpec(memory_space=pl.ANY)
    return pl.pallas_call(
        middle_kernel,
        out_shape=(
            jax.ShapeDtypeStruct((nodes, width), BF16),
            jax.ShapeDtypeStruct((nodes, width), BF16),
            jax.ShapeDtypeStruct((nodes + WIN, 2 * width), BF16),
        ),
        in_specs=[vmem, away, away, away],
        out_specs=(vmem, vmem, vmem),
        scratch_shapes=[
            pltpu.VMEM((nodes, width), BF16),
            pltpu.VMEM((width, width), BF16),
            pltpu.VMEM((width, 3 * width), BF16),
            pltpu.VMEM((half, width), BF16),
            pltpu.VMEM((half, width), BF16),
            pltpu.VMEM((nodes, width), BF16),
            pltpu.SemaphoreType.DMA((2,)),
            pltpu.SemaphoreType.DMA,
            pltpu.SemaphoreType.DMA,
            pltpu.SemaphoreType.DMA((2,)),
            pltpu.SemaphoreType.DMA((2,)),
        ],
        compiler_params=params(has_side_effects=True, collective_id=1),
        name="middle",
    )(latent, ctx, cross_out, self_qkv)


PACK = 512
SIZES = (2048, 2304, 2560, 3072, 4096)
SPARE = 2048


def lane_max(scores, width):
    top = scores[:, 0:PAIR]
    for c in range(1, width // PAIR):
        top = jnp.maximum(top, scores[:, c * PAIR : (c + 1) * PAIR])
    return top


def pack_rows(kv, packed):
    groups = kv.shape[0] // PACK
    row = lax.broadcasted_iota(jnp.int32, (PACK, PACK), 0)
    column = lax.broadcasted_iota(jnp.int32, (PACK, PACK), 1)
    slot = lax.broadcasted_iota(jnp.int32, (PACK, 2 * PAIR), 0)
    earlier = (row < column).astype(BF16)
    lives = []
    for g in range(groups):
        key = kv[g * PACK : (g + 1) * PACK, 0:PAIR].astype(F32)
        lives.append(jnp.transpose(jnp.where(key < PADDING_FROM, 1.0, 0.0))[0:1, :])
    live = jnp.concatenate(lives, axis=0)
    before = jnp.dot(live.astype(BF16), earlier, preferred_element_type=F32)
    places = jnp.where(live > 0.5, before, -1.0).astype(jnp.int32)
    end = 0
    for g in range(groups):
        number = jnp.sum(live[g : g + 1, :]).astype(jnp.int32)
        pick = (places[g : g + 1, :] == row).astype(BF16)
        found = jnp.dot(pick, kv[g * PACK : (g + 1) * PACK, :], preferred_element_type=F32)
        packed[pl.ds(pl.multiple_of(end, 16), PACK), :] = jnp.where(
            slot < number, found, PADDING
        ).astype(BF16)
        end = end + (number + 15) // 16 * 16
    packed[pl.ds(pl.multiple_of(end, 16), SPARE), :] = jnp.full((SPARE, 2 * PAIR), PADDING, BF16)
    return end


def cross_kernel(kv, q, out, packed, k0, k1, v0, v1, s0, s1, length):
    block = q.shape[0]

    @pl.when(pl.program_id(0) == 0)
    def _():
        end = pack_rows(kv, packed)
        length[0] = end
        lane = lax.broadcasted_iota(jnp.int32, (PACK, PAIR), 1)
        low = lane < HEAD

        blocks = SIZES[-1] // PACK
        for size in SIZES[-2::-1]:
            blocks = jnp.where(end <= size, -(-size // PACK), blocks)

        @pl.loop(0, blocks)
        def _(b):
            at = pl.ds(pl.multiple_of(b * PACK, PACK), PACK)
            key = packed[at, 0:PAIR].astype(F32)
            value = packed[at, PAIR:].astype(F32)
            live = key < PADDING_FROM
            bias = jnp.where(live, 0.0, MASKED)
            key = jnp.where(live, key, 0.0)
            value = jnp.where(live, value, 0.0)
            first = jnp.where(low, key, jnp.where(lane == HEAD, bias, 0.0))
            second = jnp.where(low, jnp.where(lane == 0, bias, 0.0), key)
            k0[:, at] = jnp.transpose(first).astype(BF16)
            k1[:, at] = jnp.transpose(second).astype(BF16)
            v0[at, :] = jnp.where(low, value, 1.0).astype(BF16)
            v1[at, :] = jnp.where(low, 1.0, value).astype(BF16)

    end = length[0]

    def attend(size):
        lane = lax.broadcasted_iota(jnp.int32, (block, PAIR), 1)
        low = lane < HEAD
        both = q[...].astype(F32)
        q0 = jnp.where(low, both, jnp.where(lane == HEAD, 1.0, 0.0)).astype(BF16)
        q1 = jnp.where(low, jnp.where(lane == 0, 1.0, 0.0), both).astype(BF16)
        step = 512
        chunks = [slice(at, min(at + step, size)) for at in range(0, size, step)]
        lowest = jnp.full((block, PAIR), -3e38, F32)
        zero = jnp.zeros((block, PAIR), F32)

        def score(query, k, s, at, top):
            scores = jnp.dot(query, k[:, at], preferred_element_type=F32)
            s[:, at] = scores
            return jnp.maximum(top, lane_max(scores, at.stop - at.start))

        def mix(s, v, top, at, total):
            weights = jnp.exp2(s[:, at] - top).astype(BF16)
            return total + jnp.dot(weights, v[at, :], preferred_element_type=F32)

        top0, top1, t0, t1 = lowest, lowest, zero, zero
        for at in chunks:
            top0 = score(q0, k0, s0, at, top0)
        top0 = jnp.max(top0, axis=1, keepdims=True)
        for at in chunks:
            top1 = score(q1, k1, s1, at, top1)
            t0 = mix(s0, v0, top0, at, t0)
        top1 = jnp.max(top1, axis=1, keepdims=True)
        for at in chunks:
            t1 = mix(s1, v1, top1, at, t1)
        sums = pltpu.roll(jnp.where(low, t1, t0), HEAD, 1)
        out[...] = (jnp.where(low, t0, t1) / sums).astype(BF16)

    for below, size in zip((0, *SIZES[:-1]), SIZES):
        pl.when((end > below) & (end <= size))(functools.partial(attend, size))


def cross_attention(kv, q, block=512):
    rows = kv.shape[0]
    nodes = q.shape[0]
    return pl.pallas_call(
        cross_kernel,
        grid=(nodes // block,),
        out_shape=jax.ShapeDtypeStruct(q.shape, BF16),
        in_specs=[
            pl.BlockSpec((rows, 2 * PAIR), lambda j: (0, 0)),
            pl.BlockSpec((block, PAIR), lambda j: (j, 0)),
        ],
        out_specs=pl.BlockSpec((block, PAIR), lambda j: (j, 0)),
        scratch_shapes=[
            pltpu.VMEM((rows + SPARE, 2 * PAIR), BF16),
            pltpu.VMEM((PAIR, rows), BF16),
            pltpu.VMEM((PAIR, rows), BF16),
            pltpu.VMEM((rows, PAIR), BF16),
            pltpu.VMEM((rows, PAIR), BF16),
            pltpu.VMEM((block, rows), F32),
            pltpu.VMEM((block, rows), F32),
            pltpu.SMEM((1,), jnp.int32),
        ],
        compiler_params=params(),
        name="cross_attention",
    )(kv, q)


def window_kernel(block, q, key, value, out, bias):
    nodes = q.shape[0]
    window = key.shape[0]
    half = (window - nodes) // 2
    wide = block + 2 * half
    me = (lax.axis_index("loc") * 4 + lax.axis_index("s0")) * 2 + lax.axis_index("s1")

    @pl.when(pl.program_id(0) == 0)
    def _():
        first = jnp.where(me == 0, half, 0)
        last = jnp.where(me == LOC * GROUPS - 1, half + nodes, window)
        row = lax.broadcasted_iota(jnp.int32, (block, wide), 0)
        column = lax.broadcasted_iota(jnp.int32, (block, wide), 1)
        near = (column >= row) & (column <= row + 2 * half)
        for b in range(nodes // block):
            there = (column + b * block >= first) & (column + b * block < last)
            bias[b] = jnp.where(near & there, 0.0, MASKED)

    values = value[...].astype(F32)
    low_values = lax.broadcasted_iota(jnp.int32, values.shape, 1) < HEAD
    v0 = jnp.where(low_values, values, 1.0).astype(BF16)
    v1 = jnp.where(low_values, 1.0, values).astype(BF16)
    low = lax.broadcasted_iota(jnp.int32, (block, PAIR), 1) < HEAD
    for b in range(nodes // block):
        both = q[b * block : (b + 1) * block, :].astype(F32)
        q0 = jnp.where(low, both, 0.0).astype(BF16)
        q1 = jnp.where(low, 0.0, both).astype(BF16)
        near = slice(b * block, b * block + wide)
        a0 = lax.dot_general(q0, key[near, :], NT, preferred_element_type=F32) + bias[b]
        a1 = lax.dot_general(q1, key[near, :], NT, preferred_element_type=F32) + bias[b]
        p0 = jnp.exp2(a0 - jnp.max(a0, axis=1, keepdims=True)).astype(BF16)
        p1 = jnp.exp2(a1 - jnp.max(a1, axis=1, keepdims=True)).astype(BF16)
        t0 = jnp.dot(p0, v0[near], preferred_element_type=F32)
        t1 = jnp.dot(p1, v1[near], preferred_element_type=F32)
        sums = pltpu.roll(jnp.where(low, t1, t0), HEAD, 1)
        out[b * block : (b + 1) * block, :] = (jnp.where(low, t0, t1) / sums).astype(BF16)


def window_attention(q, kv, block=192):
    nodes = q.shape[0]
    window = kv.shape[0]
    return pl.pallas_call(
        functools.partial(window_kernel, block),
        grid=(GROUPS,),
        out_shape=jax.ShapeDtypeStruct(q.shape, BF16),
        in_specs=[
            pl.BlockSpec((nodes, PAIR), lambda j: (0, j)),
            pl.BlockSpec((window, PAIR), lambda j: (0, j)),
            pl.BlockSpec((window, PAIR), lambda j: (0, j + GROUPS)),
        ],
        out_specs=pl.BlockSpec((nodes, PAIR), lambda j: (0, j)),
        scratch_shapes=[pltpu.VMEM((nodes // block, block, block + window - nodes), F32)],
        compiler_params=params(),
        name="window_attention",
    )(q, kv, kv)


def tail_kernel(
    ctx, before, self_out, weights, out,
    w_in, w_back, x, mine, other, total, part, got, w_sems, send, recv,
):
    loc = lax.axis_index("loc")
    z = lax.axis_index("s0")
    core = lax.axis_index("s1")
    chunks, devices = w_in.shape[0], w_in.shape[1]
    sibling = functools.partial(
        pltpu.make_async_remote_copy, device_id=(loc, z, 1 - core), device_id_type=MESH
    )

    def load(c):
        at = pl.ds(c * devices, devices)
        return (
            pltpu.make_async_copy(weights.at[at, 0], w_in.at[c], w_sems.at[0, c]),
            pltpu.make_async_copy(weights.at[at, 1], w_back.at[c], w_sems.at[1, c]),
        )

    for c in range(chunks):
        for copy in load(c):
            copy.start()
    barrier = pltpu.get_barrier_semaphore()
    pl.semaphore_signal(barrier, inc=1, device_id=(loc, z, 1 - core), device_id_type=MESH)

    mixed = jnp.dot(ctx[...], self_out[...], preferred_element_type=F32)
    after = (before[...].astype(F32) + mixed).astype(BF16)
    x[...] = after
    mine[...] = rms_norm(after)
    pl.semaphore_wait(barrier, 1)
    give = sibling(mine, other, send.at[0], recv.at[0])
    give.start()

    def mlp(rows, c):
        wide = devices * w_in.shape[2]
        first = w_in[c].reshape(wide, w_in.shape[3])
        second = w_back[c].reshape(wide, w_back.shape[3])
        hidden = lax.dot_general(rows[...], first, NT, preferred_element_type=F32)
        hidden = jax.nn.gelu(hidden, approximate=True).astype(BF16)
        return jnp.dot(hidden, second, preferred_element_type=F32)

    for copy in load(0):
        copy.wait()
    total[...] = mlp(mine, 0)
    give.wait_recv()
    part[...] = mlp(other, 0)
    for c in range(1, chunks):
        for copy in load(c):
            copy.wait()

    @pl.loop(1, chunks)
    def _(c):
        part[...] += mlp(other, c)

    back = sibling(part, got, send.at[1], recv.at[1])
    back.start()

    @pl.loop(1, chunks)
    def _(c):
        total[...] += mlp(mine, c)

    back.wait_recv()
    out[...] = (x[...].astype(F32) + (total[...] + got[...])).astype(BF16)
    give.wait_send()
    back.wait_send()


def tail(ctx, before, self_out, weights, chunks=4):
    nodes, width = ctx.shape
    devices, _, units, _ = weights.shape
    vmem = pl.BlockSpec(memory_space=pltpu.VMEM)
    block = (chunks, devices // chunks, units, width)
    return pl.pallas_call(
        tail_kernel,
        out_shape=jax.ShapeDtypeStruct(ctx.shape, BF16),
        in_specs=[vmem, vmem, vmem, pl.BlockSpec(memory_space=pl.ANY)],
        out_specs=vmem,
        scratch_shapes=[
            pltpu.VMEM(block, BF16),
            pltpu.VMEM(block, BF16),
            pltpu.VMEM((nodes, width), BF16),
            pltpu.VMEM((nodes, width), BF16),
            pltpu.VMEM((nodes, width), BF16),
            pltpu.VMEM((nodes, width), F32),
            pltpu.VMEM((nodes, width), F32),
            pltpu.VMEM((nodes, width), F32),
            pltpu.SemaphoreType.DMA((2, chunks)),
            pltpu.SemaphoreType.DMA((2,)),
            pltpu.SemaphoreType.DMA((2,)),
        ],
        compiler_params=params(has_side_effects=True, collective_id=3),
        name="tail",
    )(ctx, before, self_out, weights)


def shards(
    latent,
    observations,
    counts,
    cross_query,
    cross_kv,
    cross_out,
    self_qkv,
    self_out,
    mlp_in,
    mlp_out,
):
    nodes, width = latent.shape
    kv, q, column = project(
        counts.reshape(-1), observations.reshape(-1, width), latent, cross_kv, cross_query,
        mlp_in.T, mlp_out.T,
    )
    weights = lax.all_gather(column, "loc").reshape(-1, *column.shape[1:])
    kv_here, q_here = exchange(kv.reshape(LOC * GROUPS, CAP, 2 * PAIR), q)
    ctx = cross_attention(
        kv_here.reshape(-1, 2 * PAIR), q_here.reshape(-1, PAIR)
    )
    after_cross, self_q, self_kv = middle(
        latent, ctx.reshape(GROUPS, nodes, PAIR), cross_out, self_qkv
    )
    self_ctx = window_attention(self_q, self_kv)
    return tail(self_ctx, after_cross, self_out, weights)


def solution(mesh):
    finer = Mesh(mesh.devices.reshape(LOC, 4, 2), LOC_STREAM)
    return jax.shard_map(
        shards,
        mesh=finer,
        in_specs=(
            P(LOC_STREAM, None),
            P(STREAM, "loc", None, None, None),
            P(STREAM, "loc", None),
            P(),
            P(),
            P(),
            P(),
            P(),
            P(None, LOC_STREAM),
            P(None, LOC_STREAM),
        ),
        out_specs=P(LOC_STREAM, None),
        check_vma=False,
    )
```

```python
import functools
import math

import jax
import jax.numpy as jnp
from jax import lax
from jax.experimental import pallas as pl
from jax.experimental.pallas import tpu as pltpu
from jax.sharding import Mesh
from jax.sharding import PartitionSpec as P

HEADS = 16
HEAD = 64
PAIR = 128
GROUPS = 8
WIN = 512
LOC = 16
CAP = 32
STREAM = ("s0", "s1")
LOC_STREAM = ("loc", "s0", "s1")
EPSILON = 1e-06
MASKED = -1e30
PADDING = 1e30
PADDING_FROM = 1e29
QSCALE = math.log2(math.e) / math.sqrt(HEAD)
MESH = pl.DeviceIdType.MESH
F32 = jnp.float32
BF16 = jnp.bfloat16
NT = (((1,), (1,)), ((), ()))
VMEM_LIMIT = 56 << 20


def params(**more):
    return pltpu.CompilerParams(vmem_limit_bytes=VMEM_LIMIT, **more)


def rms_norm(tensor):
    floats = tensor.astype(F32)
    return (floats * lax.rsqrt(jnp.mean(floats * floats, axis=-1, keepdims=True) + EPSILON)).astype(
        BF16
    )


def project_kernel(
    counts, obs, latent, wk, wv, wq, w_in, w_back, kv_out, q_out, column,
    xn, ln, send, recv,
):
    loc = lax.axis_index("loc")
    z = lax.axis_index("s0")
    core = lax.axis_index("s1")
    step = pl.program_id(0)

    @pl.when(step == 0)
    def _():
        barrier = pltpu.get_barrier_semaphore()
        for d in range(1, 4):
            pl.semaphore_signal(
                barrier, inc=1, device_id=(loc, lax.rem(z + d, 4), core), device_id_type=MESH
            )
        xn[...] = rms_norm(obs[...])
        ln[...] = rms_norm(latent[...])

        pl.semaphore_wait(barrier, 3)
        for at, part in enumerate((w_in, w_back)):
            pltpu.make_async_copy(part, column.at[z, at], recv).start()
            for d in range(1, 4):
                pltpu.make_async_remote_copy(
                    part, column.at[z, at], send, recv,
                    device_id=(loc, lax.rem(z + d, 4), core), device_id_type=MESH,
                ).start()

    q = (jnp.dot(ln[...], wq[...], preferred_element_type=F32) * QSCALE).astype(BF16)
    k = jnp.dot(xn[...], wk[...], preferred_element_type=F32)
    v = jnp.dot(xn[...], wv[...], preferred_element_type=F32)
    slot = lax.broadcasted_iota(jnp.int32, (CAP, PAIR), 0)
    for s in range(LOC):
        live = slot < counts[s]
        rows = slice(s * CAP, (s + 1) * CAP)
        for g in range(2):
            columns = slice(g * PAIR, (g + 1) * PAIR)
            kv_out[s, g, :, 0:PAIR] = jnp.where(live, k[rows, columns], PADDING).astype(BF16)
            kv_out[s, g, :, PAIR:] = jnp.where(live, v[rows, columns], PADDING).astype(BF16)
    for g in range(2):
        q_out[g] = q[:, g * PAIR : (g + 1) * PAIR]

    @pl.when(step == pl.num_programs(0) - 1)
    def _():
        sent = column.at[pl.ds(0, 3)]
        pltpu.make_async_copy(sent, sent, send).wait()
        pltpu.make_async_copy(column, column, recv).wait()


def project(counts, obs, latent, cross_kv, cross_query, w_in, w_back):
    rows, width = obs.shape
    nodes = latent.shape[0]
    step = 2 * PAIR
    steps = width // step
    return pl.pallas_call(
        project_kernel,
        grid=(steps,),
        out_shape=(
            jax.ShapeDtypeStruct((LOC, GROUPS, CAP, 2 * PAIR), BF16),
            jax.ShapeDtypeStruct((GROUPS, nodes, PAIR), BF16),
            jax.ShapeDtypeStruct((4, 2, *w_in.shape), BF16),
        ),
        in_specs=[
            pl.BlockSpec(memory_space=pltpu.SMEM),
            pl.BlockSpec((rows, width), lambda j: (0, 0)),
            pl.BlockSpec((nodes, width), lambda j: (0, 0)),
            pl.BlockSpec((width, step), lambda j: (0, j)),
            pl.BlockSpec((width, step), lambda j: (0, j + steps)),
            pl.BlockSpec((width, step), lambda j: (0, j)),
            pl.BlockSpec(memory_space=pl.ANY),
            pl.BlockSpec(memory_space=pl.ANY),
        ],
        out_specs=(
            pl.BlockSpec((LOC, 2, CAP, 2 * PAIR), lambda j: (0, j, 0, 0)),
            pl.BlockSpec((2, nodes, PAIR), lambda j: (j, 0, 0)),
            pl.BlockSpec(memory_space=pl.ANY),
        ),
        scratch_shapes=[
            pltpu.VMEM((rows, width), BF16),
            pltpu.VMEM((nodes, width), BF16),
            pltpu.SemaphoreType.DMA,
            pltpu.SemaphoreType.DMA,
        ],
        compiler_params=params(has_side_effects=True, collective_id=2),
        name="project",
    )(counts, obs, latent, cross_kv, cross_kv, cross_query, w_in, w_back)


def exchange_kernel(kv, q, kv_here, q_here, kv_send, kv_recv, q_send, q_recv):
    loc = lax.axis_index("loc")
    me = lax.axis_index("s0") * 2 + lax.axis_index("s1")
    mine = loc * GROUPS + me
    pltpu.make_async_copy(q.at[me], q_here.at[me], q_recv).start()
    pltpu.make_async_copy(kv.at[mine], kv_here.at[me * LOC + loc], kv_recv).start()

    @pl.loop(1, GROUPS)
    def _(d):
        to = lax.rem(me + d, GROUPS)
        pltpu.make_async_remote_copy(
            q.at[to],
            q_here.at[me],
            q_send,
            q_recv,
            device_id=(loc, to // 2, lax.rem(to, 2)),
            device_id_type=MESH,
        ).start()

    @pl.loop(1, LOC * GROUPS)
    def _(d):
        to = lax.rem(mine + d * 37, LOC * GROUPS)
        section = to // GROUPS
        group = lax.rem(to, GROUPS)
        pltpu.make_async_remote_copy(
            kv.at[to],
            kv_here.at[me * LOC + loc],
            kv_send,
            kv_recv,
            device_id=(section, group // 2, lax.rem(group, 2)),
            device_id_type=MESH,
        ).start()

    pltpu.make_async_copy(q.at[pl.ds(0, GROUPS - 1)], q_here.at[pl.ds(0, GROUPS - 1)], q_send).wait()
    pltpu.make_async_copy(q, q_here, q_recv).wait()

    sent = pl.ds(0, LOC * GROUPS - 1)
    pltpu.make_async_copy(kv.at[sent], kv_here.at[sent], kv_send).wait()
    pltpu.make_async_copy(kv_here, kv_here, kv_recv).wait()


def exchange(kv, q):
    return pl.pallas_call(
        exchange_kernel,
        out_shape=(
            jax.ShapeDtypeStruct(kv.shape, BF16),
            jax.ShapeDtypeStruct(q.shape, BF16),
        ),
        in_specs=[pl.BlockSpec(memory_space=pl.ANY)] * 2,
        out_specs=(pl.BlockSpec(memory_space=pl.ANY),) * 2,
        scratch_shapes=[pltpu.SemaphoreType.DMA] * 4,
        compiler_params=params(has_side_effects=True),
        name="exchange",
    )(kv, q)


def middle_kernel(
    latent, ctx, cross_out, self_qkv, after, q, kv,
    mixed, w_out, w_qkv, halo, normed, w_sems, ctx_send, ctx_recv, send, recv,
):
    loc = lax.axis_index("loc")
    me = lax.axis_index("s0") * 2 + lax.axis_index("s1")
    flat = loc * GROUPS + me
    nodes, width = latent.shape
    half = halo.shape[1]
    low, high = halo.at[0], halo.at[1]
    starts, ends = flat == 0, flat == LOC * GROUPS - 1
    outer_low = (me == 0) & jnp.logical_not(starts)
    outer_high = (me == GROUPS - 1) & jnp.logical_not(ends)

    def device(index):
        group = lax.rem(index, GROUPS)
        return index // GROUPS, group // 2, lax.rem(group, 2)

    load_out = pltpu.make_async_copy(cross_out, w_out, w_sems.at[0])
    load_qkv = pltpu.make_async_copy(self_qkv, w_qkv, w_sems.at[1])
    load_out.start()
    load_qkv.start()

    barrier = pltpu.get_barrier_semaphore()

    @pl.loop(1, GROUPS)
    def _(d):
        to = lax.rem(me + d, GROUPS)
        pl.semaphore_signal(
            barrier, inc=1, device_id=(loc, to // 2, lax.rem(to, 2)), device_id_type=MESH
        )

    @pl.when(outer_low)
    def _():
        pl.semaphore_signal(barrier, inc=1, device_id=device(flat - 1), device_id_type=MESH)

    @pl.when(outer_high)
    def _():
        pl.semaphore_signal(barrier, inc=1, device_id=device(flat + 1), device_id_type=MESH)

    pl.semaphore_wait(
        barrier, GROUPS - 1 + outer_low.astype(jnp.int32) + outer_high.astype(jnp.int32)
    )

    place = mixed.at[:, pl.ds(pl.multiple_of(me * PAIR, PAIR), PAIR)]

    @pl.loop(1, GROUPS)
    def _(d):
        to = lax.rem(me + d, GROUPS)
        pltpu.make_async_remote_copy(
            ctx.at[to],
            place,
            ctx_send,
            ctx_recv,
            device_id=(loc, to // 2, lax.rem(to, 2)),
            device_id_type=MESH,
        ).start()

    pltpu.make_async_copy(ctx.at[me], place, ctx_recv).start()

    @pl.when(starts)
    def _():
        halo[0] = jnp.zeros(halo.shape[1:], BF16)

    @pl.when(ends)
    def _():
        halo[1] = jnp.zeros(halo.shape[1:], BF16)

    load_out.wait()
    pltpu.make_async_copy(mixed, mixed, ctx_recv).wait()
    after[...] = (
        latent[...].astype(F32) + jnp.dot(mixed[...], w_out[...], preferred_element_type=F32)
    ).astype(BF16)

    down = pltpu.make_async_remote_copy(
        after.at[0:half], high, send.at[0], recv.at[1],
        device_id=device(jnp.maximum(flat - 1, 0)), device_id_type=MESH,
    )
    up = pltpu.make_async_remote_copy(
        after.at[nodes - half : nodes], low, send.at[1], recv.at[0],
        device_id=device(jnp.minimum(flat + 1, LOC * GROUPS - 1)), device_id_type=MESH,
    )
    pl.when(jnp.logical_not(starts))(down.start)
    pl.when(jnp.logical_not(ends))(up.start)

    normed[...] = rms_norm(after[...])
    load_qkv.wait()
    step = 512

    @pl.loop(0, width // step)
    def _(c):
        at = pl.ds(pl.multiple_of(c * step, step), step)
        found = jnp.dot(normed[...], w_qkv[:, at], preferred_element_type=F32)
        q[:, at] = (found * QSCALE).astype(BF16)

    def project(rows, to):
        @pl.loop(0, 2 * width // step)
        def _(c):
            at = pl.ds(pl.multiple_of(c * step, step), step)
            weights = w_qkv[:, pl.ds(pl.multiple_of(width + c * step, step), step)]
            kv[to, at] = jnp.dot(rows[...], weights, preferred_element_type=F32).astype(BF16)

    project(normed, slice(half, half + nodes))

    core = lax.axis_index("s1")

    @pl.loop(0, 2)
    def _(i):
        side = lax.rem(1 - core + i, 2)
        come = ((side == 0) & jnp.logical_not(starts)) | ((side == 1) & jnp.logical_not(ends))

        @pl.when(come)
        def _():
            pltpu.make_async_copy(halo.at[side], halo.at[side], recv.at[side]).wait()

        normed[0:half] = rms_norm(halo[side])
        first = pl.multiple_of(side * (half + nodes), PAIR)
        project(normed.at[0:half], pl.ds(first, half))

    pl.when(jnp.logical_not(starts))(down.wait_send)
    pl.when(jnp.logical_not(ends))(up.wait_send)
    sent = ctx.at[pl.ds(0, GROUPS - 1)]
    pltpu.make_async_copy(sent, sent, ctx_send).wait()


def middle(latent, ctx, cross_out, self_qkv):
    nodes, width = latent.shape
    half = WIN // 2
    vmem = pl.BlockSpec(memory_space=pltpu.VMEM)
    away = pl.BlockSpec(memory_space=pl.ANY)
    return pl.pallas_call(
        middle_kernel,
        out_shape=(
            jax.ShapeDtypeStruct((nodes, width), BF16),
            jax.ShapeDtypeStruct((nodes, width), BF16),
            jax.ShapeDtypeStruct((nodes + WIN, 2 * width), BF16),
        ),
        in_specs=[vmem, away, away, away],
        out_specs=(vmem, vmem, vmem),
        scratch_shapes=[
            pltpu.VMEM((nodes, width), BF16),
            pltpu.VMEM((width, width), BF16),
            pltpu.VMEM((width, 3 * width), BF16),
            pltpu.VMEM((2, half, width), BF16),
            pltpu.VMEM((nodes, width), BF16),
            pltpu.SemaphoreType.DMA((2,)),
            pltpu.SemaphoreType.DMA,
            pltpu.SemaphoreType.DMA,
            pltpu.SemaphoreType.DMA((2,)),
            pltpu.SemaphoreType.DMA((2,)),
        ],
        compiler_params=params(has_side_effects=True, collective_id=1),
        name="middle",
    )(latent, ctx, cross_out, self_qkv)


PACK = 512
SIZES = (2048, 2304, 2560, 3072, 4096)
SPARE = 2048


def lane_max(scores, width):
    top = scores[:, 0:PAIR]
    for c in range(1, width // PAIR):
        top = jnp.maximum(top, scores[:, c * PAIR : (c + 1) * PAIR])
    return top


def pack_rows(kv, packed):
    groups = kv.shape[0] // PACK
    row = lax.broadcasted_iota(jnp.int32, (PACK, PACK), 0)
    column = lax.broadcasted_iota(jnp.int32, (PACK, PACK), 1)
    slot = lax.broadcasted_iota(jnp.int32, (PACK, 2 * PAIR), 0)
    earlier = (row < column).astype(BF16)
    lives = []
    for g in range(groups):
        key = kv[g * PACK : (g + 1) * PACK, 0:PAIR].astype(F32)
        lives.append(jnp.transpose(jnp.where(key < PADDING_FROM, 1.0, 0.0))[0:1, :])
    live = jnp.concatenate(lives, axis=0)
    before = jnp.dot(live.astype(BF16), earlier, preferred_element_type=F32)
    places = jnp.where(live > 0.5, before, -1.0).astype(jnp.int32)
    end = 0
    for g in range(groups):
        number = jnp.sum(live[g : g + 1, :]).astype(jnp.int32)
        pick = (places[g : g + 1, :] == row).astype(BF16)
        found = jnp.dot(pick, kv[g * PACK : (g + 1) * PACK, :], preferred_element_type=F32)
        packed[pl.ds(pl.multiple_of(end, 16), PACK), :] = jnp.where(
            slot < number, found, PADDING
        ).astype(BF16)
        end = end + (number + 15) // 16 * 16
    packed[pl.ds(pl.multiple_of(end, 16), SPARE), :] = jnp.full((SPARE, 2 * PAIR), PADDING, BF16)
    return end


def cross_kernel(kv, q, out, packed, k0, k1, v0, v1, s0, s1, length):
    block = q.shape[0]

    @pl.when(pl.program_id(0) == 0)
    def _():
        end = pack_rows(kv, packed)
        length[0] = end
        lane = lax.broadcasted_iota(jnp.int32, (PACK, PAIR), 1)
        low = lane < HEAD

        blocks = SIZES[-1] // PACK
        for size in SIZES[-2::-1]:
            blocks = jnp.where(end <= size, -(-size // PACK), blocks)

        @pl.loop(0, blocks)
        def _(b):
            at = pl.ds(pl.multiple_of(b * PACK, PACK), PACK)
            key = packed[at, 0:PAIR].astype(F32)
            value = packed[at, PAIR:].astype(F32)
            live = key < PADDING_FROM
            bias = jnp.where(live, 0.0, MASKED)
            key = jnp.where(live, key, 0.0)
            value = jnp.where(live, value, 0.0)
            first = jnp.where(low, key, jnp.where(lane == HEAD, bias, 0.0))
            second = jnp.where(low, jnp.where(lane == 0, bias, 0.0), key)
            k0[:, at] = jnp.transpose(first).astype(BF16)
            k1[:, at] = jnp.transpose(second).astype(BF16)
            v0[at, :] = jnp.where(low, value, 1.0).astype(BF16)
            v1[at, :] = jnp.where(low, 1.0, value).astype(BF16)

    end = length[0]

    def attend(size):
        lane = lax.broadcasted_iota(jnp.int32, (block, PAIR), 1)
        low = lane < HEAD
        both = q[...].astype(F32)
        q0 = jnp.where(low, both, jnp.where(lane == HEAD, 1.0, 0.0)).astype(BF16)
        q1 = jnp.where(low, jnp.where(lane == 0, 1.0, 0.0), both).astype(BF16)
        step = 512
        chunks = [slice(at, min(at + step, size)) for at in range(0, size, step)]
        lowest = jnp.full((block, PAIR), -3e38, F32)
        zero = jnp.zeros((block, PAIR), F32)

        def score(query, k, s, at, top):
            scores = jnp.dot(query, k[:, at], preferred_element_type=F32)
            s[:, at] = scores
            return jnp.maximum(top, lane_max(scores, at.stop - at.start))

        def mix(s, v, top, at, total):
            weights = jnp.exp2(s[:, at] - top).astype(BF16)
            return total + jnp.dot(weights, v[at, :], preferred_element_type=F32)

        top0, top1, t0, t1 = lowest, lowest, zero, zero
        for at in chunks:
            top0 = score(q0, k0, s0, at, top0)
        top0 = jnp.max(top0, axis=1, keepdims=True)
        for at in chunks:
            top1 = score(q1, k1, s1, at, top1)
            t0 = mix(s0, v0, top0, at, t0)
        top1 = jnp.max(top1, axis=1, keepdims=True)
        for at in chunks:
            t1 = mix(s1, v1, top1, at, t1)
        sums = pltpu.roll(jnp.where(low, t1, t0), HEAD, 1)
        out[...] = (jnp.where(low, t0, t1) / sums).astype(BF16)

    for below, size in zip((0, *SIZES[:-1]), SIZES):
        pl.when((end > below) & (end <= size))(functools.partial(attend, size))


def cross_attention(kv, q, block=512):
    rows = kv.shape[0]
    nodes = q.shape[0]
    return pl.pallas_call(
        cross_kernel,
        grid=(nodes // block,),
        out_shape=jax.ShapeDtypeStruct(q.shape, BF16),
        in_specs=[
            pl.BlockSpec((rows, 2 * PAIR), lambda j: (0, 0)),
            pl.BlockSpec((block, PAIR), lambda j: (j, 0)),
        ],
        out_specs=pl.BlockSpec((block, PAIR), lambda j: (j, 0)),
        scratch_shapes=[
            pltpu.VMEM((rows + SPARE, 2 * PAIR), BF16),
            pltpu.VMEM((PAIR, rows), BF16),
            pltpu.VMEM((PAIR, rows), BF16),
            pltpu.VMEM((rows, PAIR), BF16),
            pltpu.VMEM((rows, PAIR), BF16),
            pltpu.VMEM((block, rows), F32),
            pltpu.VMEM((block, rows), F32),
            pltpu.SMEM((1,), jnp.int32),
        ],
        compiler_params=params(),
        name="cross_attention",
    )(kv, q)


def window_kernel(block, q, key, value, out, bias):
    nodes = q.shape[0]
    window = key.shape[0]
    half = (window - nodes) // 2
    wide = block + 2 * half
    me = (lax.axis_index("loc") * 4 + lax.axis_index("s0")) * 2 + lax.axis_index("s1")

    @pl.when(pl.program_id(0) == 0)
    def _():
        first = jnp.where(me == 0, half, 0)
        last = jnp.where(me == LOC * GROUPS - 1, half + nodes, window)
        row = lax.broadcasted_iota(jnp.int32, (block, wide), 0)
        column = lax.broadcasted_iota(jnp.int32, (block, wide), 1)
        near = (column >= row) & (column <= row + 2 * half)
        for b in range(nodes // block):
            there = (column + b * block >= first) & (column + b * block < last)
            bias[b] = jnp.where(near & there, 0.0, MASKED)

    values = value[...].astype(F32)
    low_values = lax.broadcasted_iota(jnp.int32, values.shape, 1) < HEAD
    v0 = jnp.where(low_values, values, 1.0).astype(BF16)
    v1 = jnp.where(low_values, 1.0, values).astype(BF16)
    low = lax.broadcasted_iota(jnp.int32, (block, PAIR), 1) < HEAD
    for b in range(nodes // block):
        both = q[b * block : (b + 1) * block, :].astype(F32)
        q0 = jnp.where(low, both, 0.0).astype(BF16)
        q1 = jnp.where(low, 0.0, both).astype(BF16)
        near = slice(b * block, b * block + wide)
        a0 = lax.dot_general(q0, key[near, :], NT, preferred_element_type=F32) + bias[b]
        a1 = lax.dot_general(q1, key[near, :], NT, preferred_element_type=F32) + bias[b]
        p0 = jnp.exp2(a0 - jnp.max(a0, axis=1, keepdims=True)).astype(BF16)
        p1 = jnp.exp2(a1 - jnp.max(a1, axis=1, keepdims=True)).astype(BF16)
        t0 = jnp.dot(p0, v0[near], preferred_element_type=F32)
        t1 = jnp.dot(p1, v1[near], preferred_element_type=F32)
        sums = pltpu.roll(jnp.where(low, t1, t0), HEAD, 1)
        out[b * block : (b + 1) * block, :] = (jnp.where(low, t0, t1) / sums).astype(BF16)


def window_attention(q, kv, block=192):
    nodes = q.shape[0]
    window = kv.shape[0]
    return pl.pallas_call(
        functools.partial(window_kernel, block),
        grid=(GROUPS,),
        out_shape=jax.ShapeDtypeStruct(q.shape, BF16),
        in_specs=[
            pl.BlockSpec((nodes, PAIR), lambda j: (0, j)),
            pl.BlockSpec((window, PAIR), lambda j: (0, j)),
            pl.BlockSpec((window, PAIR), lambda j: (0, j + GROUPS)),
        ],
        out_specs=pl.BlockSpec((nodes, PAIR), lambda j: (0, j)),
        scratch_shapes=[pltpu.VMEM((nodes // block, block, block + window - nodes), F32)],
        compiler_params=params(),
        name="window_attention",
    )(q, kv, kv)


def tail_kernel(
    ctx, before, self_out, weights, out,
    w_in, w_back, x, mine, other, total, part, got, w_sems, send, recv,
):
    loc = lax.axis_index("loc")
    z = lax.axis_index("s0")
    core = lax.axis_index("s1")
    chunks, devices = w_in.shape[0], w_in.shape[1]
    sibling = functools.partial(
        pltpu.make_async_remote_copy, device_id=(loc, z, 1 - core), device_id_type=MESH
    )

    def load(c):
        at = pl.ds(c * devices, devices)
        return (
            pltpu.make_async_copy(weights.at[at, 0], w_in.at[c], w_sems.at[0, c]),
            pltpu.make_async_copy(weights.at[at, 1], w_back.at[c], w_sems.at[1, c]),
        )

    for c in range(chunks):
        for copy in load(c):
            copy.start()
    barrier = pltpu.get_barrier_semaphore()
    pl.semaphore_signal(barrier, inc=1, device_id=(loc, z, 1 - core), device_id_type=MESH)

    mixed = jnp.dot(ctx[...], self_out[...], preferred_element_type=F32)
    after = (before[...].astype(F32) + mixed).astype(BF16)
    x[...] = after
    mine[...] = rms_norm(after)
    pl.semaphore_wait(barrier, 1)
    give = sibling(mine, other, send.at[0], recv.at[0])
    give.start()

    def mlp(rows, c):
        wide = devices * w_in.shape[2]
        first = w_in[c].reshape(wide, w_in.shape[3])
        second = w_back[c].reshape(wide, w_back.shape[3])
        hidden = lax.dot_general(rows[...], first, NT, preferred_element_type=F32)
        hidden = jax.nn.gelu(hidden, approximate=True).astype(BF16)
        return jnp.dot(hidden, second, preferred_element_type=F32)

    for copy in load(0):
        copy.wait()
    total[...] = mlp(mine, 0)
    give.wait_recv()
    part[...] = mlp(other, 0)
    for c in range(1, chunks):
        for copy in load(c):
            copy.wait()

    @pl.loop(1, chunks)
    def _(c):
        part[...] += mlp(other, c)

    back = sibling(part, got, send.at[1], recv.at[1])
    back.start()

    @pl.loop(1, chunks)
    def _(c):
        total[...] += mlp(mine, c)

    back.wait_recv()
    out[...] = (x[...].astype(F32) + (total[...] + got[...])).astype(BF16)
    give.wait_send()
    back.wait_send()


def tail(ctx, before, self_out, weights, chunks=4):
    nodes, width = ctx.shape
    devices, _, units, _ = weights.shape
    vmem = pl.BlockSpec(memory_space=pltpu.VMEM)
    block = (chunks, devices // chunks, units, width)
    return pl.pallas_call(
        tail_kernel,
        out_shape=jax.ShapeDtypeStruct(ctx.shape, BF16),
        in_specs=[vmem, vmem, vmem, pl.BlockSpec(memory_space=pl.ANY)],
        out_specs=vmem,
        scratch_shapes=[
            pltpu.VMEM(block, BF16),
            pltpu.VMEM(block, BF16),
            pltpu.VMEM((nodes, width), BF16),
            pltpu.VMEM((nodes, width), BF16),
            pltpu.VMEM((nodes, width), BF16),
            pltpu.VMEM((nodes, width), F32),
            pltpu.VMEM((nodes, width), F32),
            pltpu.VMEM((nodes, width), F32),
            pltpu.SemaphoreType.DMA((2, chunks)),
            pltpu.SemaphoreType.DMA((2,)),
            pltpu.SemaphoreType.DMA((2,)),
        ],
        compiler_params=params(has_side_effects=True, collective_id=3),
        name="tail",
    )(ctx, before, self_out, weights)


def shards(
    latent,
    observations,
    counts,
    cross_query,
    cross_kv,
    cross_out,
    self_qkv,
    self_out,
    mlp_in,
    mlp_out,
):
    nodes, width = latent.shape
    kv, q, column = project(
        counts.reshape(-1), observations.reshape(-1, width), latent, cross_kv, cross_query,
        mlp_in.T, mlp_out.T,
    )
    weights = lax.all_gather(column, "loc").reshape(-1, *column.shape[1:])
    kv_here, q_here = exchange(kv.reshape(LOC * GROUPS, CAP, 2 * PAIR), q)
    ctx = cross_attention(
        kv_here.reshape(-1, 2 * PAIR), q_here.reshape(-1, PAIR)
    )
    after_cross, self_q, self_kv = middle(
        latent, ctx.reshape(GROUPS, nodes, PAIR), cross_out, self_qkv
    )
    self_ctx = window_attention(self_q, self_kv)
    return tail(self_ctx, after_cross, self_out, weights)


def solution(mesh):
    finer = Mesh(mesh.devices.reshape(LOC, 4, 2), LOC_STREAM)
    return jax.shard_map(
        shards,
        mesh=finer,
        in_specs=(
            P(LOC_STREAM, None),
            P(STREAM, "loc", None, None, None),
            P(STREAM, "loc", None),
            P(),
            P(),
            P(),
            P(),
            P(),
            P(None, LOC_STREAM),
            P(None, LOC_STREAM),
        ),
        out_specs=P(LOC_STREAM, None),
        check_vma=False,
    )
```
